32 devices in a mesh: dp: 16 (over z, y, x), tensor: 2 (over core).
Axes of the slice: x: 2, y: 2, z: 4, core: 2. Of those that a mesh axis runs over, the one named last changes fastest.
Arguments:
- tokens: bfloat16 [8192, 1024], P(('dp', 'tensor')), may hold values from -6 to 6
- teacher: bfloat16 [8192, 1024], P(('dp', 'tensor')), may hold values from -6 to 6
- lengths: int32 [16], P('dp'), may hold values from 128 to 512, as said below
- w_qkv: bfloat16 [1024, 3, 1024], P('dp', None, 'tensor'), may hold values from -0.1875 to 0.1875
- w_out: bfloat16 [1024, 1024], P('dp', 'tensor'), may hold values from -0.1875 to 0.1875
- w_up: bfloat16 [1024, 4096], P('dp', 'tensor'), may hold values from -0.1875 to 0.1875
- w_down: bfloat16 [1024, 4096], P('dp', 'tensor'), may hold values from -0.09375 to 0.09375
- norm_gain: float32 [4, 1024], replicated, may hold values from 0.5 to 1.5
- norm_bias: float32 [4, 1024], replicated, may hold values from -3 to 3
Outputs:
- loss: float32 [], replicated
- layer_output: bfloat16 [8192, 1024], P(('dp', 'tensor'))
- tokens_grad: float32 [8192, 1024], P(('dp', 'tensor'))
- w_qkv_grad: float32 [1024, 3, 1024], P('dp', None, 'tensor')
- w_out_grad: float32 [1024, 1024], P('dp', 'tensor')
- w_up_grad: float32 [1024, 4096], P('dp', 'tensor')
- w_down_grad: float32 [1024, 4096], P('dp', 'tensor')
- gain_grad: float32 [4, 1024], P(None, ('dp', 'tensor'))
- bias_grad: float32 [4, 1024], P(None, ('dp', 'tensor'))
The draws below stay inside these ranges and needn't reach their ends.
Inputs may be any that keep to these rules, and one draw needn't show every extreme that they name: Each row's valid slots are its first lengths[r] slots.
All inputs are finite; a program needn't handle non-finite values.
Results may differ from the reference program's by a relative error of at most 0.015.
Values may be sent and summed in bfloat16 or wider, within the bound.
No kernel may reach another device: no remote copies, remote signals or barrier semaphores. Data moves between devices by JAX's collectives and lax.ppermute only.
A program may use at most 128 MiB of HBM per device.

```python
import jax
import jax.numpy as jnp
from jax import lax

D = 1024
HEADS = 16
HEAD_DIM = 64
FF = 4096
SLOTS = 512
ROWS_ALL = 16
TOKENS = 8192
N_TENSOR = 2


def draw_lengths(key, part):
    row_ids = jnp.arange(ROWS_ALL).astype(jnp.int32)
    last_row = max(ROWS_ALL - 1, 1)
    least = SLOTS // 4
    floor_rows = least + SLOTS // 4 * row_ids // last_row
    ceiling_rows = least + 3 * SLOTS // 4 * row_ids // last_row
    values = jax.random.randint(key, (ROWS_ALL,), floor_rows, ceiling_rows + 1)
    values = jnp.where(row_ids == 0, least, values)
    values = jnp.where(row_ids == ROWS_ALL - 1, SLOTS, values)
    return values.astype(jnp.int32)


def level_of(key, shape, pieces, low, high):
    def one(dim, shards_of):
        steps = jax.random.uniform(jax.random.fold_in(jax.random.fold_in(key, 6), dim), (shards_of,), jnp.float32, low / len(pieces), high / len(pieces))
        return jnp.repeat(jnp.exp(steps), shape[dim] // shards_of).reshape((-1,) + (1,) * (len(shape) - dim - 1))

    level = one(*pieces[0])
    for cut in pieces[1:]:
        level = level * one(*cut)
    return level


def gaussian(rng, dims, width, bound, split=(), dtype=jnp.bfloat16):
    entries = width * jax.random.normal(rng, dims, jnp.float32)
    if split:
        entries = entries * level_of(rng, dims, split, -0.22, 0.18)
    return jnp.clip(entries, -bound, bound).astype(dtype)


def setup_inputs(seed: int = 0) -> dict:
    seeds = jax.random.split(jax.random.key(seed), 10)
    return {
        "tokens": gaussian(seeds[0], (TOKENS, D), 1.0, 6.0, ((0, 32),)),
        "teacher": gaussian(seeds[1], (TOKENS, D), 1.0, 6.0, ((0, 32),)),
        "lengths": draw_lengths(jax.random.fold_in(seeds[9], 71), 0),
        "w_qkv": gaussian(seeds[3], (D, 3, D), D ** -0.5, 0.1875, ((0, 16), (2, 2))),
        "w_out": gaussian(seeds[4], (D, D), D ** -0.5, 0.1875, ((0, 16), (1, 2))),
        "w_up": gaussian(seeds[5], (D, FF), D ** -0.5, 0.1875, ((0, 16), (1, 2))),
        "w_down": gaussian(seeds[6], (D, FF), FF ** -0.5, 0.09375, ((0, 16), (1, 2))),
        "norm_gain": jnp.clip(1.0 + 0.1 * jax.random.normal(seeds[7], (4, D), jnp.float32), 0.5, 1.5),
        "norm_bias": gaussian(seeds[8], (4, D), 0.2, 3.0, (), jnp.float32),
    }


@jax.custom_vjp
def low(v):
    return lax.optimization_barrier(v.astype(jnp.bfloat16)).astype(jnp.float32)

@jax.custom_vjp
def low_back(v):
    return v

def low_keep(v):
    return (low(v), None)

def low_pass(kept, grad):
    return (grad,)

def back_keep(v):
    return (v, None)

def back_low(kept, grad):
    return (low(grad),)
low.defvjp(low_keep, low_pass)
low_back.defvjp(back_keep, back_low)
norm_eps = 1e-05
highest = lax.Precision.HIGHEST

def layer_norm(values, gain, shift):
    center = values - lax.optimization_barrier(jnp.mean(values, axis=-1, keepdims=True))
    spread = lax.optimization_barrier(jnp.mean(center * center, axis=-1, keepdims=True))
    return center * lax.rsqrt(spread + norm_eps) * gain + shift

def rotary_tables(slot_count, head_size):
    places = jnp.arange(slot_count).astype(jnp.float32)
    freqs = 10000.0 ** (-2.0 * jnp.arange(head_size // 2).astype(jnp.float32) / head_size)
    angles = places[:, None] * freqs[None, :]
    return (jnp.cos(angles)[:, None, :], jnp.sin(angles)[:, None, :])

def rotate_pairs(values, cosine, sine):
    half_size = values.shape[-1] // 2
    front = values[..., :half_size]
    back_half = values[..., half_size:]
    return jnp.concatenate([front * cosine - back_half * sine, back_half * cosine + front * sine], axis=-1)

def attend_row(queries, key_rows, value_rows, length):
    slot_count = queries.shape[0]
    scores = jnp.einsum('qhd,khd->hqk', queries, key_rows, precision=highest) * HEAD_DIM ** (-0.5)
    scores = low_back(scores)
    places = jnp.arange(slot_count).astype(jnp.int32)
    allowed = (places[None, :] <= places[:, None]) & (places[None, :] < length)
    scores = jnp.where(allowed[None], scores, -1000000000.0)
    top_score = lax.optimization_barrier(jnp.max(scores, axis=-1, keepdims=True))
    weights = jnp.exp(scores - top_score)
    weights = low(weights / lax.optimization_barrier(jnp.sum(weights, axis=-1, keepdims=True)))
    return jnp.einsum('hqk,khd->qhd', weights, value_rows, precision=highest)
checked_row = jax.checkpoint(attend_row)

def group_sum(inputs, weight_t):
    token_count, inner = inputs.shape
    split_in = inputs.reshape(token_count, N_TENSOR, inner // N_TENSOR)
    split_weight = weight_t.reshape(weight_t.shape[0], N_TENSOR, inner // N_TENSOR)
    partials = jnp.einsum('tgk,dgk->gtd', split_in, split_weight, precision=highest)
    return lax.optimization_barrier(jnp.sum(low(partials), axis=0))

def reference(tokens, teacher, lengths, w_qkv, w_out, w_up, w_down, norm_gain, norm_bias):
    places = jnp.arange(SLOTS).astype(jnp.int32)
    valid = (places[None, :] < lengths[:, None]).astype(jnp.float32).reshape(TOKENS, 1)
    count = jnp.sum(valid)
    target = teacher.astype(jnp.float32)
    cosine, sine = rotary_tables(SLOTS, HEAD_DIM)

    def forward(inputs, weight_qkv, weight_out, weight_up, weight_down, gains, shifts):
        normed_one = low(layer_norm(inputs, gains[0], shifts[0]))
        mixed = low_back(jnp.einsum('td,dcf->tcf', normed_one, weight_qkv, precision=highest))
        mixed = mixed.reshape(ROWS_ALL, SLOTS, 3, HEADS, HEAD_DIM)
        queries = low(rotate_pairs(mixed[:, :, 0], cosine, sine))
        key_rows = low(rotate_pairs(mixed[:, :, 1], cosine, sine))
        value_rows = low(mixed[:, :, 2])
        attended = lax.map(lambda packed: checked_row(*packed), (queries, key_rows, value_rows, lengths))
        attended = low(low_back(attended.reshape(TOKENS, D)))
        attn_sum = low_back(group_sum(attended, weight_out))
        middle = inputs + layer_norm(attn_sum, gains[1], shifts[1])
        normed_two = low(layer_norm(middle, gains[2], shifts[2]))
        hidden = low_back(jnp.dot(normed_two, weight_up, precision=highest))
        active = low(jax.nn.gelu(hidden, approximate=False))
        mlp_sum = low_back(group_sum(active, weight_down))
        result = middle + layer_norm(mlp_sum, gains[3], shifts[3])
        error = result - target
        squared = jnp.sum(valid * error * error)
        return (squared * (TOKENS / (2.0 * count)), (result, squared))
    floats = (tokens.astype(jnp.float32), w_qkv.astype(jnp.float32), w_out.astype(jnp.float32), w_up.astype(jnp.float32), w_down.astype(jnp.float32), norm_gain, norm_bias)
    objective, pullback, extras = jax.vjp(forward, *floats, has_aux=True)
    grads = pullback(jnp.ones_like(objective))
    result, squared = extras
    loss = squared / (count * D)
    return (loss, result.astype(jnp.bfloat16), grads[0], grads[1], grads[2], grads[3], grads[4], grads[5], grads[6])
```

```python
import jax
import jax.numpy as jnp
from jax import lax
from jax.sharding import PartitionSpec as P

HEAD_DIM = 64


norm_eps = 1e-05


def norm_stats(values):
    center = values - jnp.mean(values, axis=-1, keepdims=True)
    spread = jnp.mean(center * center, axis=-1, keepdims=True)
    inv = lax.rsqrt(spread + norm_eps)
    return center * inv, inv


def norm_back(grad, normal, inv, gain):
    e = grad * gain
    back = inv * (
        e
        - jnp.mean(e, axis=-1, keepdims=True)
        - normal * jnp.mean(e * normal, axis=-1, keepdims=True)
    )
    return back, jnp.sum(grad * normal, axis=0), jnp.sum(grad, axis=0)


def rotary_tables(slot_count, head_size):
    places = jnp.arange(slot_count).astype(jnp.float32)
    freqs = 10000.0 ** (-2.0 * jnp.arange(head_size // 2).astype(jnp.float32) / head_size)
    angles = places[:, None] * freqs[None, :]
    return (jnp.cos(angles)[:, None, :], jnp.sin(angles)[:, None, :])


def rotate_pairs(values, cosine, sine):
    half_size = values.shape[-1] // 2
    front = values[..., :half_size]
    back_half = values[..., half_size:]
    return jnp.concatenate(
        [front * cosine - back_half * sine, back_half * cosine + front * sine], axis=-1
    )


def allowed_pairs(begin, block, key_count, length):
    key_places = jnp.arange(key_count)
    query_places = begin + jnp.arange(block)
    return (key_places[None, :] <= query_places[:, None]) & (key_places[None, :] < length)


def attend_forward(packed):
    queries, key_rows, value_rows, length = packed
    slot_count = queries.shape[0]
    block = min(512, slot_count)
    scale = HEAD_DIM ** (-0.5)
    outputs = []
    totals = []
    for begin in range(0, slot_count, block):
        finish = begin + block
        scores = (
            jnp.einsum(
                "qhd,khd->hqk",
                queries[begin:finish],
                key_rows[:finish],
                preferred_element_type=jnp.float32,
            )
            * scale
        )
        allowed = allowed_pairs(begin, block, finish, length)
        scores = jnp.where(allowed[None], scores, -1000000000.0)
        top_score = jnp.max(scores, axis=-1, keepdims=True)
        weights = jnp.exp(scores - top_score)
        weight_sum = jnp.sum(weights, axis=-1, keepdims=True)
        probs = (weights / weight_sum).astype(jnp.bfloat16)
        outputs.append(
            jnp.einsum(
                "hqk,khd->qhd", probs, value_rows[:finish], preferred_element_type=jnp.float32
            )
        )
        totals.append((top_score + jnp.log(weight_sum))[:, :, 0])
    return (jnp.concatenate(outputs, axis=0), jnp.concatenate(totals, axis=1))


def attend_backward(packed):
    queries, key_rows, value_rows, outputs, out_grads, totals, length = packed
    slot_count = queries.shape[0]
    block = min(512, slot_count)
    scale = HEAD_DIM ** (-0.5)
    delta = jnp.sum(out_grads.astype(jnp.float32) * outputs, axis=-1).T
    key_grads = jnp.zeros(key_rows.shape, jnp.float32)
    value_grads = jnp.zeros(value_rows.shape, jnp.float32)
    query_grads = []
    for begin in range(0, slot_count, block):
        finish = begin + block
        query_block = queries[begin:finish]
        grad_block = out_grads[begin:finish]
        key_part = key_rows[:finish]
        value_part = value_rows[:finish]
        scores = (
            jnp.einsum("qhd,khd->hqk", query_block, key_part, preferred_element_type=jnp.float32)
            * scale
        )
        allowed = allowed_pairs(begin, block, finish, length)
        probs = jnp.where(allowed[None], jnp.exp(scores - totals[:, begin:finish, None]), 0.0)
        value_grads = value_grads.at[:finish].add(
            jnp.einsum(
                "hqk,qhd->khd",
                probs.astype(jnp.bfloat16),
                grad_block,
                preferred_element_type=jnp.float32,
            )
        )
        prob_grads = jnp.einsum(
            "qhd,khd->hqk", grad_block, value_part, preferred_element_type=jnp.float32
        )
        score_grads = (probs * (prob_grads - delta[:, begin:finish, None])).astype(jnp.bfloat16)
        query_grads.append(
            jnp.einsum("hqk,khd->qhd", score_grads, key_part, preferred_element_type=jnp.float32)
            * scale
        )
        key_grads = key_grads.at[:finish].add(
            jnp.einsum("hqk,qhd->khd", score_grads, query_block, preferred_element_type=jnp.float32)
            * scale
        )
    return (jnp.concatenate(query_grads, axis=0), key_grads, value_grads)


def swap(values, bit):
    size = lax.axis_size("dp")
    return lax.ppermute(values, "dp", [(j, j ^ (1 << bit)) for j in range(size)])


def swap_core(values):
    return lax.ppermute(values, "tensor", [(0, 1), (1, 0)])


def add_low(*terms):
    total = terms[0].astype(jnp.float32)
    for term in terms[1:]:
        total = total + term.astype(jnp.float32)
    return total


def low(values):
    return values.astype(jnp.bfloat16)


def bit_order(members):
    bits = members.bit_length() - 1
    return (1, 0) + tuple(range(bits - 1, 1, -1))


def relative_map(members, width):
    order = bit_order(members)
    block = width // members
    rel = jnp.arange(width)
    place = rel // block
    mask = jnp.zeros_like(rel)
    for k, bit in enumerate(order):
        mask = mask | (((place >> (len(order) - 1 - k)) & 1) << bit)
    source = (lax.axis_index("dp") ^ mask) * block + rel % block
    return (jnp.arange(width)[:, None] == source[None, :]).astype(jnp.bfloat16)


def gather_rows(part):
    bits = lax.axis_size("dp").bit_length() - 1
    own = part
    for bit in range(2, bits):
        own = jnp.concatenate([own, swap(own, bit)], axis=0)
    half = own.shape[1] // 2
    over_x = swap(own, 0)
    over_y = swap(own, 1)
    corner = jnp.concatenate([swap(over_x[:, :half], 1), swap(over_y[:, half:], 0)], axis=1)
    return jnp.concatenate([own, over_x, over_y, corner], axis=0)


def scatter_rows(blocks):
    here, over_x, over_y, corner = blocks
    bits = lax.axis_size("dp").bit_length() - 1
    half = here.shape[1] // 2
    from_y = swap(corner[:, :half], 1)
    from_x = swap(corner[:, half:], 0)
    to_x = jnp.concatenate([low(add_low(over_x[:, :half], from_y)), over_x[:, half:]], axis=1)
    to_y = jnp.concatenate([over_y[:, :half], low(add_low(over_y[:, half:], from_x))], axis=1)
    got_x = swap(to_x, 0)
    got_y = swap(to_y, 1)
    terms = [here, got_x, got_y]
    for bit in range(bits - 1, 1, -1):
        cut = terms[0].shape[0] // 2
        got = swap(low(add_low(*[t[cut:] for t in terms])), bit)
        terms = [low(add_low(*[t[:cut] for t in terms])), got]
    return add_low(*terms)


def grad_blocks(left, right):
    step = left.shape[1] // 4
    outs = [
        low(
            lax.dot_general(
                left[:, k * step : (k + 1) * step],
                right,
                (((0,), (0,)), ((), ())),
                preferred_element_type=jnp.float32,
            )
        )
        for k in (3, 1, 2, 0)
    ]
    return outs[3], outs[1], outs[2], outs[0]


def collect_rows(values):
    groups = lax.axis_size("tensor")
    if groups != 2:
        return lax.all_gather(values, "tensor", axis=0, tiled=True)
    other = swap_core(values)
    first = lax.axis_index("tensor") == 0
    return jnp.concatenate(
        [jnp.where(first, values, other), jnp.where(first, other, values)], axis=0
    )


def product_reduce(inputs, weight, dims, own_rows):
    groups = lax.axis_size("tensor")

    def product(rows):
        return low(lax.dot_general(rows, weight, dims, preferred_element_type=jnp.float32))

    if groups != 2:
        return lax.psum_scatter(
            product(inputs), "tensor", scatter_dimension=0, tiled=True
        ).astype(jnp.float32)
    me = lax.axis_index("tensor")
    away = product(lax.dynamic_slice_in_dim(inputs, (1 - me) * own_rows, own_rows, 0))
    got = swap_core(away)
    mine = product(lax.dynamic_slice_in_dim(inputs, me * own_rows, own_rows, 0))
    return add_low(mine, got)


def on_device(tokens, teacher, lengths, w_qkv, w_out, w_up, w_down, norm_gain, norm_bias):
    tok_dev, width = tokens.shape
    groups = lax.axis_size("tensor")
    members = lax.axis_size("dp")
    bits = members.bit_length() - 1
    row_count = lengths.shape[0]
    group_tokens = tok_dev * groups
    slot_count = group_tokens // row_count
    all_slots = group_tokens * members
    me = lax.axis_index("tensor")
    places = me * tok_dev + jnp.arange(tok_dev)
    row_index = places // slot_count
    row_length = jnp.sum(
        jnp.where(row_index[:, None] == jnp.arange(row_count)[None, :], lengths[None, :], 0), axis=1
    )
    valid = (places % slot_count < row_length).astype(jnp.float32)[:, None]
    cosine, sine = rotary_tables(slot_count, HEAD_DIM)
    local_width = w_qkv.shape[2]
    heads_here = local_width // HEAD_DIM
    out_width = w_out.shape[1]
    hidden_width = w_up.shape[1]

    weight_qkv = gather_rows(w_qkv.reshape(w_qkv.shape[0], 3 * local_width))
    joined = gather_rows(jnp.concatenate([w_out, w_up], axis=1))
    weight_out, weight_up = joined[:, :out_width], joined[:, out_width:]
    weight_down = gather_rows(w_down)

    count = jnp.sum(lengths).astype(jnp.float32).reshape(1, 1)
    for bit in range(bits):
        count = count + swap(count, bit)

    to_rel = relative_map(members, width)

    def relative(values):
        return jnp.dot(values, to_rel, preferred_element_type=jnp.float32)

    def absolute(values, precision=None):
        return lax.dot_general(
            values,
            to_rel.astype(values.dtype),
            (((1,), (1,)), ((), ())),
            precision=precision,
            preferred_element_type=jnp.float32,
        )

    inputs = relative(tokens)
    target = relative(teacher)
    affine = jnp.dot(
        jnp.concatenate([norm_gain, norm_bias], axis=0),
        to_rel.astype(jnp.float32),
        precision=lax.Precision.HIGHEST,
        preferred_element_type=jnp.float32,
    )
    gain, bias = affine[:4], affine[4:]

    normal_zero, inv_zero = norm_stats(inputs)
    rows_one = collect_rows(low(normal_zero * gain[0] + bias[0]))
    mixed = jnp.dot(rows_one, weight_qkv, preferred_element_type=jnp.float32)
    mixed = mixed.reshape(row_count, slot_count, 3, heads_here, HEAD_DIM)
    queries = low(rotate_pairs(mixed[:, :, 0], cosine, sine))
    key_rows = low(rotate_pairs(mixed[:, :, 1], cosine, sine))
    value_rows = low(mixed[:, :, 2])
    attended, totals = lax.map(attend_forward, (queries, key_rows, value_rows, lengths))
    attended_low = low(attended.reshape(group_tokens, local_width))
    across = (((1,), (1,)), ((), ()))
    attn_sum = product_reduce(attended_low, weight_out, across, tok_dev)
    normal_one, inv_one = norm_stats(attn_sum)
    middle = inputs + normal_one * gain[1] + bias[1]
    normal_two, inv_two = norm_stats(middle)
    rows_two = collect_rows(low(normal_two * gain[2] + bias[2]))
    hidden = jnp.dot(rows_two, weight_up, preferred_element_type=jnp.float32)
    gate = 0.5 * (1.0 + lax.erf(hidden * (2.0**-0.5)))
    active = low(hidden * gate)
    slope = low(gate + hidden * jnp.exp(-0.5 * hidden * hidden) * ((2.0 * jnp.pi) ** -0.5))
    mlp_sum = product_reduce(active, weight_down, across, tok_dev)
    normal_three, inv_three = norm_stats(mlp_sum)
    result = middle + normal_three * gain[3] + bias[3]
    error = result - target
    squared = jnp.sum(valid * error * error)
    out_grad = valid * error * (all_slots / count)

    mlp_grad, gain_three, bias_three = norm_back(out_grad, normal_three, inv_three, gain[3])
    mlp_rows = collect_rows(low(mlp_grad))
    down_part = scatter_rows(grad_blocks(mlp_rows, active))
    active_grad = jnp.dot(mlp_rows, weight_down, preferred_element_type=jnp.float32)
    hidden_grad = low(active_grad * slope.astype(jnp.float32))
    up_part = scatter_rows(grad_blocks(rows_two, hidden_grad))
    normed_two_grad = product_reduce(hidden_grad, weight_up, across, tok_dev)
    middle_extra, gain_two, bias_two = norm_back(normed_two_grad, normal_two, inv_two, gain[2])
    middle_grad = out_grad + middle_extra
    attn_grad, gain_one, bias_one = norm_back(middle_grad, normal_one, inv_one, gain[1])
    attn_rows = collect_rows(low(attn_grad))
    attended_grad = low(jnp.dot(attn_rows, weight_out, preferred_element_type=jnp.float32))
    out_part = scatter_rows(grad_blocks(attn_rows, attended_low))
    attended_grad = attended_grad.reshape(row_count, slot_count, heads_here, HEAD_DIM)
    query_grads, key_grads, value_grads = lax.map(
        attend_backward, (queries, key_rows, value_rows, attended, attended_grad, totals, lengths)
    )
    mixed_grad = jnp.stack(
        [
            rotate_pairs(query_grads, cosine, -sine),
            rotate_pairs(key_grads, cosine, -sine),
            value_grads,
        ],
        axis=2,
    )
    mixed_grad = low(mixed_grad.reshape(group_tokens, 3 * local_width))
    qkv_part = scatter_rows(grad_blocks(rows_one, mixed_grad))
    normed_one_grad = product_reduce(mixed_grad, weight_qkv, across, tok_dev)
    input_extra, gain_zero, bias_zero = norm_back(normed_one_grad, normal_zero, inv_zero, gain[0])
    tokens_grad = absolute(middle_grad + input_extra, lax.Precision.HIGHEST)

    sums = jnp.stack(
        [
            gain_zero, gain_one, gain_two, gain_three,
            bias_zero, bias_one, bias_two, bias_three,
        ],
        axis=0,
    )
    total = jnp.broadcast_to(squared, (8, 128))
    if groups == 2:
        got = swap_core(jnp.concatenate([sums, total], axis=1))
        sums, total = sums + got[:, :width], total + got[:, width:]
    else:
        sums, total = lax.psum((sums, total), "tensor")
    for bit in bit_order(members):
        cut = sums.shape[1] // 2
        got = swap(jnp.concatenate([sums[:, cut:], total], axis=1), bit)
        sums, total = sums[:, :cut] + got[:, :cut], total + got[:, cut:]
    loss = total[0, 0] / (count[0, 0] * width)
    own = sums.shape[1] // groups
    sums = lax.dynamic_slice_in_dim(sums, me * own, own, 1)
    return (
        loss,
        low(absolute(low(result))),
        tokens_grad,
        qkv_part.reshape(w_qkv.shape),
        out_part,
        up_part,
        down_part,
        sums[:4],
        sums[4:],
    )


def solution(mesh):
    return jax.shard_map(
        on_device,
        mesh=mesh,
        in_specs=(
            P(("dp", "tensor"), None),
            P(("dp", "tensor"), None),
            P("dp"),
            P("dp", None, "tensor"),
            P("dp", "tensor"),
            P("dp", "tensor"),
            P("dp", "tensor"),
            P(),
            P(),
        ),
        out_specs=(
            P(),
            P(("dp", "tensor"), None),
            P(("dp", "tensor"), None),
            P("dp", None, "tensor"),
            P("dp", "tensor"),
            P("dp", "tensor"),
            P("dp", "tensor"),
            P(None, ("dp", "tensor")),
            P(None, ("dp", "tensor")),
        ),
        check_vma=False,
    )
```

```python
import jax
import jax.numpy as jnp
from jax import lax
from jax.sharding import PartitionSpec as P

HEAD_DIM = 64


norm_eps = 1e-05


def norm_stats(values):
    center = values - jnp.mean(values, axis=-1, keepdims=True)
    spread = jnp.mean(center * center, axis=-1, keepdims=True)
    inv = lax.rsqrt(spread + norm_eps)
    return center * inv, inv


def norm_back(grad, normal, inv, gain):
    e = grad * gain
    back = inv * (
        e
        - jnp.mean(e, axis=-1, keepdims=True)
        - normal * jnp.mean(e * normal, axis=-1, keepdims=True)
    )
    return back, jnp.sum(grad * normal, axis=0), jnp.sum(grad, axis=0)


def rotary_tables(slot_count, head_size):
    places = jnp.arange(slot_count).astype(jnp.float32)
    freqs = 10000.0 ** (-2.0 * jnp.arange(head_size // 2).astype(jnp.float32) / head_size)
    angles = places[:, None] * freqs[None, :]
    return (jnp.cos(angles)[:, None, :], jnp.sin(angles)[:, None, :])


def rotate_pairs(values, cosine, sine):
    half_size = values.shape[-1] // 2
    front = values[..., :half_size]
    back_half = values[..., half_size:]
    return jnp.concatenate(
        [front * cosine - back_half * sine, back_half * cosine + front * sine], axis=-1
    )


def allowed_pairs(begin, block, key_count, length):
    key_places = jnp.arange(key_count)
    query_places = begin + jnp.arange(block)
    return (key_places[None, :] <= query_places[:, None]) & (key_places[None, :] < length)


def attend_forward(packed):
    queries, key_rows, value_rows, length = packed
    slot_count = queries.shape[0]
    block = min(512, slot_count)
    scale = HEAD_DIM ** (-0.5)
    outputs = []
    totals = []
    for begin in range(0, slot_count, block):
        finish = begin + block
        scores = (
            jnp.einsum(
                "qhd,khd->hqk",
                queries[begin:finish],
                key_rows[:finish],
                preferred_element_type=jnp.float32,
            )
            * scale
        )
        allowed = allowed_pairs(begin, block, finish, length)
        scores = jnp.where(allowed[None], scores, -1000000000.0)
        top_score = jnp.max(scores, axis=-1, keepdims=True)
        weights = jnp.exp(scores - top_score)
        weight_sum = jnp.sum(weights, axis=-1, keepdims=True)
        probs = (weights / weight_sum).astype(jnp.bfloat16)
        outputs.append(
            jnp.einsum(
                "hqk,khd->qhd", probs, value_rows[:finish], preferred_element_type=jnp.float32
            )
        )
        totals.append((top_score + jnp.log(weight_sum))[:, :, 0])
    return (jnp.concatenate(outputs, axis=0), jnp.concatenate(totals, axis=1))


def attend_backward(packed):
    queries, key_rows, value_rows, outputs, out_grads, totals, length = packed
    slot_count = queries.shape[0]
    block = min(512, slot_count)
    scale = HEAD_DIM ** (-0.5)
    delta = jnp.sum(out_grads.astype(jnp.float32) * outputs, axis=-1).T
    key_grads = jnp.zeros(key_rows.shape, jnp.float32)
    value_grads = jnp.zeros(value_rows.shape, jnp.float32)
    query_grads = []
    for begin in range(0, slot_count, block):
        finish = begin + block
        query_block = queries[begin:finish]
        grad_block = out_grads[begin:finish]
        key_part = key_rows[:finish]
        value_part = value_rows[:finish]
        scores = (
            jnp.einsum("qhd,khd->hqk", query_block, key_part, preferred_element_type=jnp.float32)
            * scale
        )
        allowed = allowed_pairs(begin, block, finish, length)
        probs = jnp.where(allowed[None], jnp.exp(scores - totals[:, begin:finish, None]), 0.0)
        value_grads = value_grads.at[:finish].add(
            jnp.einsum(
                "hqk,qhd->khd",
                probs.astype(jnp.bfloat16),
                grad_block,
                preferred_element_type=jnp.float32,
            )
        )
        prob_grads = jnp.einsum(
            "qhd,khd->hqk", grad_block, value_part, preferred_element_type=jnp.float32
        )
        score_grads = (probs * (prob_grads - delta[:, begin:finish, None])).astype(jnp.bfloat16)
        query_grads.append(
            jnp.einsum("hqk,khd->qhd", score_grads, key_part, preferred_element_type=jnp.float32)
            * scale
        )
        key_grads = key_grads.at[:finish].add(
            jnp.einsum("hqk,qhd->khd", score_grads, query_block, preferred_element_type=jnp.float32)
            * scale
        )
    return (jnp.concatenate(query_grads, axis=0), key_grads, value_grads)


def swap(values, bit):
    size = lax.axis_size("dp")
    return lax.ppermute(values, "dp", [(j, j ^ (1 << bit)) for j in range(size)])


def swap_core(values):
    return lax.ppermute(values, "tensor", [(0, 1), (1, 0)])


def add_low(*terms):
    total = terms[0].astype(jnp.float32)
    for term in terms[1:]:
        total = total + term.astype(jnp.float32)
    return total


def low(values):
    return values.astype(jnp.bfloat16)


def after(values, *others):
    return lax.optimization_barrier((values,) + others)[0]


def relative_map(members, width):
    bits = members.bit_length() - 1
    block = width // members
    half = block // 2
    rel = jnp.arange(width)
    place = rel // half
    mask = jnp.zeros_like(rel)
    for k, bit in enumerate(range(bits - 1, 1, -1)):
        mask = mask | (((place >> k) & 1) << bit)
    side = (place >> (bits - 2)) & 1
    mask = mask | ((place >> (bits - 1)) & 3)
    source = (lax.axis_index("dp") ^ mask) * block + side * half + rel % half
    return (jnp.arange(width)[:, None] == source[None, :]).astype(jnp.bfloat16)


def high_bits():
    return tuple(range(lax.axis_size("dp").bit_length() - 2, 1, -1))


def as_halves(part):
    return part.reshape(2, part.shape[0] // 2, part.shape[1])


def as_rows(part):
    return part.reshape(-1, part.shape[-1])


def gather_z(part, first=(), last=()):
    steps = [part]
    bits = high_bits()
    for bit in bits:
        others = (first if bit == bits[0] else ()) + (last if bit == bits[-1] else ())
        own = after(steps[-1], *others) if others else steps[-1]
        steps.append(jnp.concatenate([own, swap(own, bit)], axis=1))
    return steps


def gather_sides(own):
    return swap(own, 0), swap(own, 1)


def gather_corners(sides, *others):
    over_x, over_y = sides
    cut = over_x.shape[0] // 2
    one, two = over_x[:cut], over_y[cut:]
    if others:
        one, two = after(one, *others), after(two, *others)
    return swap(one, 1), swap(two, 0)


def join_rows(*pieces):
    return lax.optimization_barrier(jnp.concatenate(pieces, axis=0))


def add_z(terms):
    for bit in reversed(high_bits()):
        cut = terms[0].shape[1] // 2
        got = swap(low(add_low(*[t[:, cut:] for t in terms])), bit)
        terms = [low(add_low(*[t[:, :cut] for t in terms])), got]
    return add_low(*terms)


def scatter_corners(corner):
    cut = corner.shape[0] // 2
    return swap(corner[:cut], 1), swap(corner[cut:], 0)


def add_corners(over_x, over_y, corners):
    from_y, from_x = corners
    cut = over_x.shape[0] // 2
    over_x = jnp.concatenate([low(add_low(over_x[:cut], from_y)), over_x[cut:]], axis=0)
    over_y = jnp.concatenate([over_y[:cut], low(add_low(over_y[cut:], from_x))], axis=0)
    return over_x, over_y


def gather_sides_of(over_x, over_y):
    return swap(over_x, 0), swap(over_y, 1)


def columns(left, *which):
    step = left.shape[1] // 8
    parts = [left[:, k * step : (k + 1) * step] for k in which]
    return jnp.concatenate(parts, axis=1)


def quarter(left, k):
    step = left.shape[1] // 4
    return left[:, k * step : (k + 1) * step]


def product_t(left, right):
    return low(
        lax.dot_general(left, right, (((0,), (0,)), ((), ())), preferred_element_type=jnp.float32)
    )


def collect_rows(values):
    groups = lax.axis_size("tensor")
    if groups != 2:
        return lax.all_gather(values, "tensor", axis=0, tiled=True)
    other = swap_core(values)
    first = lax.axis_index("tensor") == 0
    return jnp.concatenate(
        [jnp.where(first, values, other), jnp.where(first, other, values)], axis=0
    )


def product_reduce(inputs, weight, dims, own_rows):
    groups = lax.axis_size("tensor")

    def product(rows):
        return low(lax.dot_general(rows, weight, dims, preferred_element_type=jnp.float32))

    if groups != 2:
        return lax.psum_scatter(
            product(inputs), "tensor", scatter_dimension=0, tiled=True
        ).astype(jnp.float32)
    me = lax.axis_index("tensor")
    away = product(lax.dynamic_slice_in_dim(inputs, (1 - me) * own_rows, own_rows, 0))
    got = swap_core(away)
    mine = product(lax.dynamic_slice_in_dim(inputs, me * own_rows, own_rows, 0))
    return add_low(mine, got)


def on_device(tokens, teacher, lengths, w_qkv, w_out, w_up, w_down, norm_gain, norm_bias):
    tok_dev, width = tokens.shape
    groups = lax.axis_size("tensor")
    members = lax.axis_size("dp")
    bits = members.bit_length() - 1
    row_count = lengths.shape[0]
    group_tokens = tok_dev * groups
    slot_count = group_tokens // row_count
    all_slots = group_tokens * members
    me = lax.axis_index("tensor")
    places = me * tok_dev + jnp.arange(tok_dev)
    row_index = places // slot_count
    row_length = jnp.sum(
        jnp.where(row_index[:, None] == jnp.arange(row_count)[None, :], lengths[None, :], 0), axis=1
    )
    valid = (places % slot_count < row_length).astype(jnp.float32)[:, None]
    cosine, sine = rotary_tables(slot_count, HEAD_DIM)
    local_width = w_qkv.shape[2]
    heads_here = local_width // HEAD_DIM
    out_width = w_out.shape[1]
    hidden_width = w_up.shape[1]

    one = gather_z(as_halves(w_qkv.reshape(w_qkv.shape[0], 3 * local_width)))
    three_a, three_b = as_halves(w_down)
    three = jnp.stack([three_a, swap(three_a, 0), three_b, swap(three_b, 1)], axis=0)
    tokens, teacher, norm_gain, norm_bias = lax.optimization_barrier(
        (tokens, teacher, norm_gain, norm_bias, one[1])
    )[:4]
    two = as_halves(jnp.concatenate([w_out, w_up], axis=1))
    two = gather_z(two, (one[1],), (one[-1],))
    one = as_rows(one[-1])
    one_sides = gather_sides(one)
    one_corners = gather_corners(one_sides)
    three = gather_z(three, (two[1],), one_corners)
    weight_qkv = join_rows(one, *one_sides, *one_corners)
    two = after(as_rows(two[-1]), *one_corners)
    two_sides = gather_sides(two)

    to_rel = relative_map(members, width)

    def relative(values):
        return jnp.dot(values, to_rel, preferred_element_type=jnp.float32)

    def absolute(values, precision=None):
        return lax.dot_general(
            values,
            to_rel.astype(values.dtype),
            (((1,), (1,)), ((), ())),
            precision=precision,
            preferred_element_type=jnp.float32,
        )

    inputs = relative(tokens)
    target = relative(teacher)
    affine = jnp.dot(
        jnp.concatenate([norm_gain, norm_bias], axis=0),
        to_rel.astype(jnp.float32),
        precision=lax.Precision.HIGHEST,
        preferred_element_type=jnp.float32,
    )
    gain, bias = affine[:4], affine[4:]

    normal_zero, inv_zero = norm_stats(inputs)
    rows_one = collect_rows(low(normal_zero * gain[0] + bias[0]))
    mixed = jnp.dot(rows_one, weight_qkv, preferred_element_type=jnp.float32)
    mixed = mixed.reshape(row_count, slot_count, 3, heads_here, HEAD_DIM)
    queries = low(rotate_pairs(mixed[:, :, 0], cosine, sine))
    key_rows = low(rotate_pairs(mixed[:, :, 1], cosine, sine))
    value_rows = low(mixed[:, :, 2])
    attended, totals = lax.map(attend_forward, (queries, key_rows, value_rows, lengths))
    attended_low = low(attended.reshape(group_tokens, local_width))
    two_corners = gather_corners(two_sides, attended_low)
    weight_mid = join_rows(two, *two_sides, *two_corners)
    weight_out, weight_up = weight_mid[:, :out_width], weight_mid[:, out_width:]
    three = after(three[-1], attended_low, *two_sides)
    three_last = swap(three[:2], 1), swap(three[2:], 0)
    across = (((1,), (1,)), ((), ()))
    attn_sum = product_reduce(attended_low, weight_out, across, tok_dev)
    normal_one, inv_one = norm_stats(attn_sum)
    middle = inputs + normal_one * gain[1] + bias[1]
    normal_two, inv_two = norm_stats(middle)
    rows_two = collect_rows(low(normal_two * gain[2] + bias[2]))
    hidden = jnp.dot(rows_two, weight_up, preferred_element_type=jnp.float32)
    gate = 0.5 * (1.0 + lax.erf(hidden * (2.0**-0.5)))
    active = low(hidden * gate)
    slope = low(gate + hidden * jnp.exp(-0.5 * hidden * hidden) * ((2.0 * jnp.pi) ** -0.5))
    active, slope = lax.optimization_barrier((active, slope))
    (y_a0, y_a1), (x_b0, x_b1) = lax.optimization_barrier(three_last + (active,))[:2]
    weight_down = join_rows(three[0], three[2], three[1], x_b0, y_a0, three[3], y_a1, x_b1)
    mlp_sum = product_reduce(active, weight_down, across, tok_dev)
    normal_three, inv_three = norm_stats(mlp_sum)
    result = middle + normal_three * gain[3] + bias[3]
    error = result - target
    squared = jnp.sum(valid * error * error)
    out_grad = valid * error

    mlp_grad, gain_three, bias_three = norm_back(out_grad, normal_three, inv_three, gain[3])
    mlp_rows = collect_rows(low(mlp_grad))
    away = [product_t(columns(mlp_rows, k), active) for k in (4, 3)]
    early = swap(away[0], 1), swap(away[1], 0)
    left = after(mlp_rows, *away)
    away = [product_t(columns(left, k), active) for k in (6, 7)]
    late = swap(away[0], 1), swap(away[1], 0)
    left = after(mlp_rows, *away)
    down_kept = [product_t(columns(left, k), active) for k in (0, 2, 1, 5)]
    active_grad = jnp.dot(after(mlp_rows, *down_kept), weight_down, preferred_element_type=jnp.float32)
    hidden_grad = low(active_grad * slope.astype(jnp.float32))
    normed_two_grad = product_reduce(hidden_grad, weight_up, across, tok_dev)
    two_blocks = [product_t(quarter(rows_two, k), hidden_grad) for k in range(4)]
    normed_two_grad, *early = lax.optimization_barrier((normed_two_grad, *early))
    middle_extra, gain_two, bias_two = norm_back(normed_two_grad, normal_two, inv_two, gain[2])
    middle_grad = out_grad + middle_extra
    attn_grad, gain_one, bias_one = norm_back(middle_grad, normal_one, inv_one, gain[1])
    attn_rows = collect_rows(low(attn_grad))
    two_corners = scatter_corners(two_blocks[3])
    attn_rows, *late = lax.optimization_barrier((attn_rows, *late))
    down = jnp.stack(
        [low(add_low(k, g)) for k, g in zip(down_kept, (early[0], late[0], early[1], late[1]))], axis=0
    )
    two_x, two_y = two_blocks[1:3]
    attended_grad = low(jnp.dot(attn_rows, weight_out, preferred_element_type=jnp.float32))
    attended_grad = attended_grad.reshape(row_count, slot_count, heads_here, HEAD_DIM)
    down = add_z([down])
    two_x, two_y = add_corners(two_x, two_y, two_corners)
    attended_grad = after(attended_grad, two_x, two_y)
    two_sides = gather_sides_of(two_x, two_y)
    query_grads, key_grads, value_grads = lax.map(
        attend_backward, (queries, key_rows, value_rows, attended, attended_grad, totals, lengths)
    )
    mixed_grad = jnp.stack(
        [
            rotate_pairs(query_grads, cosine, -sine),
            rotate_pairs(key_grads, cosine, -sine),
            value_grads,
        ],
        axis=2,
    )
    mixed_grad = low(mixed_grad.reshape(group_tokens, 3 * local_width))

    def one_block(k):
        return jnp.concatenate(
            [
                product_t(quarter(attn_rows, k), attended_low),
                product_t(quarter(rows_one, k), mixed_grad),
            ],
            axis=1,
        )

    one_blocks = [one_block(k) for k in range(4)]
    normed_one_grad = product_reduce(after(mixed_grad, *one_blocks), weight_qkv, across, tok_dev)
    one_corner, *two_sides = lax.optimization_barrier((one_blocks[3], *two_sides))
    one_corners = scatter_corners(one_corner)
    two = add_z([as_halves(t) for t in (two_blocks[0], *two_sides)])
    one_x, one_y = add_corners(one_blocks[1], one_blocks[2], one_corners)
    one_sides = gather_sides_of(one_x, one_y)
    one = add_z([as_halves(t) for t in (one_blocks[0], *one_sides)])
    down_a = down[0] + swap(low(down[1]), 0).astype(jnp.float32)
    down_b = down[2] + swap(low(down[3]), 1).astype(jnp.float32)
    down_part = jnp.concatenate([down_a, down_b], axis=0)
    up_part, one = as_rows(two), as_rows(one)
    out_part, qkv_part = one[:, :out_width], one[:, out_width:]
    input_extra, gain_zero, bias_zero = norm_back(normed_one_grad, normal_zero, inv_zero, gain[0])
    tokens_grad = absolute(middle_grad + input_extra, lax.Precision.HIGHEST)

    sums = jnp.stack(
        [
            gain_zero, gain_one, gain_two, gain_three,
            bias_zero, bias_one, bias_two, bias_three,
        ],
        axis=0,
    )
    total = jnp.concatenate(
        [jnp.broadcast_to(squared, (4, 128)), jnp.broadcast_to(jnp.sum(valid), (4, 128))], axis=0
    )
    sums = after(sums, *one_sides)
    if groups == 2:
        got = swap_core(jnp.concatenate([sums, total], axis=1))
        sums, total = sums + got[:, :width], total + got[:, width:]
    else:
        sums, total = lax.psum((sums, total), "tensor")
    for bit in (1, 0) + high_bits()[::-1]:
        cut = sums.shape[1] // 2
        if bit == 2:
            sums = jnp.concatenate([sums[:, :cut], sums[:, cut:]], axis=0)
            total = jnp.concatenate([total, total], axis=0)
            cut = cut // 2
        got = swap(jnp.concatenate([sums[:, cut:], total], axis=1), bit)
        sums, total = sums[:, :cut] + got[:, :cut], total + got[:, cut:]
    sums = jnp.concatenate([sums[:8], sums[8:]], axis=1)
    count = total[4, 0]
    scale = all_slots / count
    loss = total[0, 0] / (count * width)
    own = sums.shape[1] // groups
    sums = lax.dynamic_slice_in_dim(sums, me * own, own, 1) * scale
    return (
        loss,
        low(absolute(low(result))),
        tokens_grad * scale,
        (qkv_part * scale).reshape(w_qkv.shape),
        out_part * scale,
        up_part * scale,
        down_part * scale,
        sums[:4],
        sums[4:],
    )


def solution(mesh):
    return jax.shard_map(
        on_device,
        mesh=mesh,
        in_specs=(
            P(("dp", "tensor"), None),
            P(("dp", "tensor"), None),
            P("dp"),
            P("dp", None, "tensor"),
            P("dp", "tensor"),
            P("dp", "tensor"),
            P("dp", "tensor"),
            P(),
            P(),
        ),
        out_specs=(
            P(),
            P(("dp", "tensor"), None),
            P(("dp", "tensor"), None),
            P("dp", None, "tensor"),
            P("dp", "tensor"),
            P("dp", "tensor"),
            P("dp", "tensor"),
            P(None, ("dp", "tensor")),
            P(None, ("dp", "tensor")),
        ),
        check_vma=False,
    )
```

```python
import jax
import jax.numpy as jnp
from jax import lax
from jax.experimental import pallas as pl
from jax.experimental.pallas import tpu as pltpu
from jax.sharding import PartitionSpec as P

HEAD_DIM = 64


norm_eps = 1e-05


def norm_stats(values):
    center = values - jnp.mean(values, axis=-1, keepdims=True)
    spread = jnp.mean(center * center, axis=-1, keepdims=True)
    inv = lax.rsqrt(spread + norm_eps)
    return center * inv, inv


def norm_back(grad, normal, inv, gain):
    e = grad * gain
    back = inv * (
        e
        - jnp.mean(e, axis=-1, keepdims=True)
        - normal * jnp.mean(e * normal, axis=-1, keepdims=True)
    )
    return back, jnp.sum(grad * normal, axis=0), jnp.sum(grad, axis=0)


def rotate_pairs(values, cosine, sine):
    half_size = values.shape[-1] // 2
    front = values[..., :half_size]
    back_half = values[..., half_size:]
    return jnp.concatenate(
        [front * cosine - back_half * sine, back_half * cosine + front * sine], axis=-1
    )


def attend_forward(packed):
    queries, key_rows, value_rows, length, places = packed
    slot_count = queries.shape[0]
    block = min(512, slot_count)
    scale = HEAD_DIM ** (-0.5)
    outputs = []
    totals = []
    for begin in range(0, slot_count, block):
        finish = begin + block
        scores = (
            jnp.einsum(
                "qhd,khd->hqk",
                queries[begin:finish],
                key_rows,
                preferred_element_type=jnp.float32,
            )
            * scale
        )
        allowed = (places[None, :] <= places[begin:finish, None]) & (places[None, :] < length)
        scores = jnp.where(allowed[None], scores, -1000000000.0)
        top_score = jnp.max(scores, axis=-1, keepdims=True)
        weights = jnp.exp(scores - top_score)
        weight_sum = jnp.sum(weights, axis=-1, keepdims=True)
        probs = (weights / weight_sum).astype(jnp.bfloat16)
        outputs.append(
            jnp.einsum("hqk,khd->qhd", probs, value_rows, preferred_element_type=jnp.float32)
        )
        totals.append((top_score + jnp.log(weight_sum))[:, :, 0])
    return (jnp.concatenate(outputs, axis=0), jnp.concatenate(totals, axis=1))


def attend_backward(packed, step, mark):
    queries, key_rows, value_rows, outputs, out_grads, totals, length, places = packed
    slot_count = queries.shape[0]
    block = min(512, slot_count)
    scale = HEAD_DIM ** (-0.5)
    delta = jnp.sum(out_grads.astype(jnp.float32) * outputs, axis=-1).T
    key_grads = 0.0
    value_grads = 0.0
    query_grads = []

    def product(form, left, right):
        left, right = step(left, right)
        return mark(jnp.einsum(form, left, right, preferred_element_type=jnp.float32))

    for begin in range(0, slot_count, block):
        finish = begin + block
        query_block = queries[begin:finish]
        grad_block = step(out_grads[begin:finish])
        scores = (
            jnp.einsum("qhd,khd->hqk", query_block, key_rows, preferred_element_type=jnp.float32)
            * scale
        )
        allowed = (places[None, :] <= places[begin:finish, None]) & (places[None, :] < length)
        probs = jnp.where(allowed[None], jnp.exp(scores - totals[:, begin:finish, None]), 0.0)
        prob_grads = jnp.einsum(
            "qhd,khd->hqk", grad_block, value_rows, preferred_element_type=jnp.float32
        )
        score_grads = mark(
            (probs * (prob_grads - delta[:, begin:finish, None])).astype(jnp.bfloat16)
        )
        value_grads = value_grads + product(
            "hqk,qhd->khd", probs.astype(jnp.bfloat16), grad_block
        )
        query_grads.append(product("hqk,khd->qhd", score_grads, key_rows) * scale)
        key_grads = key_grads + product("hqk,qhd->khd", score_grads, query_block) * scale
    return (jnp.concatenate(query_grads, axis=0), key_grads, value_grads)


def swap(values, bit):
    size = lax.axis_size("dp")
    return lax.ppermute(values, "dp", [(j, j ^ (1 << bit)) for j in range(size)])


def swap_core(values):
    return lax.ppermute(values, "tensor", [(0, 1), (1, 0)])


def add_low(*terms):
    total = terms[0].astype(jnp.float32)
    for term in terms[1:]:
        total = total + term.astype(jnp.float32)
    return total


def low(values):
    return values.astype(jnp.bfloat16)


def after(values, *others):
    return lax.optimization_barrier((values,) + others)[0]


def matmul_t(rows, weight, first, tile=256):
    count, depth = rows.shape
    outs = weight.shape[0]

    def kernel(rows_ref, weight_ref, out_ref):
        out_ref[...] = low(
            lax.dot_general(
                rows_ref[...],
                weight_ref[:, first : first + depth],
                (((1,), (1,)), ((), ())),
                preferred_element_type=jnp.float32,
            )
        )

    return pl.pallas_call(
        kernel,
        grid=(outs // tile,),
        in_specs=[
            pl.BlockSpec((count, depth), lambda j: (0, 0)),
            pl.BlockSpec((tile, weight.shape[1]), lambda j: (j, 0)),
        ],
        out_specs=pl.BlockSpec((count, tile), lambda j: (0, j)),
        out_shape=jax.ShapeDtypeStruct((count, outs), jnp.bfloat16),
        compiler_params=pltpu.CompilerParams(vmem_limit_bytes=16 * 1024 * 1024),
        cost_estimate=pl.CostEstimate(
            flops=2 * count * depth * outs, bytes_accessed=2 * outs * depth, transcendentals=0
        ),
    )(rows, weight)


def last_norm(mine, got, middle, target, valid, gain, bias):
    count, width = middle.shape
    chunk = 16
    share = 1.0 / width

    def kernel(mine_ref, got_ref, middle_ref, target_ref, valid_ref, gain_ref, bias_ref, *outs):
        result_ref, grad_ref, back_ref, sums_ref = outs
        sums_ref[...] = jnp.zeros_like(sums_ref)
        gains = gain_ref[...]

        def body(i, carry):
            rows = pl.ds(pl.multiple_of(i * chunk, chunk), chunk)
            values = add_low(mine_ref[rows, :], got_ref[rows, :])
            center = values - jnp.sum(values, axis=-1, keepdims=True) * share
            spread = jnp.sum(center * center, axis=-1, keepdims=True) * share
            inv = lax.rsqrt(spread + norm_eps)
            normal = center * inv
            result = middle_ref[rows, :] + normal * gains + bias_ref[...]
            result_ref[rows, :] = low(result)
            error = result - target_ref[rows, :].astype(jnp.float32)
            grad = valid_ref[rows, :] * error
            grad_ref[rows, :] = grad
            e = grad * gains
            turned = grad * normal
            mean_one = jnp.sum(e, axis=-1, keepdims=True) * share
            mean_two = jnp.sum(turned * gains, axis=-1, keepdims=True) * share
            back_ref[rows, :] = low(inv * (e - mean_one - normal * mean_two))
            for k, term in enumerate((turned, grad, grad * error)):
                sums_ref[8 * k : 8 * k + 8, :] += term[:8] + term[8:]
            return carry

        lax.fori_loop(0, count // chunk, body, 0, unroll=4)

    return pl.pallas_call(
        kernel,
        in_specs=[pl.BlockSpec(memory_space=pltpu.VMEM)] * 7,
        out_specs=[pl.BlockSpec(memory_space=pltpu.VMEM)] * 4,
        out_shape=[
            jax.ShapeDtypeStruct((count, width), jnp.bfloat16),
            jax.ShapeDtypeStruct((count, width), jnp.float32),
            jax.ShapeDtypeStruct((count, width), jnp.bfloat16),
            jax.ShapeDtypeStruct((24, width), jnp.float32),
        ],
        compiler_params=pltpu.CompilerParams(vmem_limit_bytes=8 * 1024 * 1024),
        cost_estimate=pl.CostEstimate(
            flops=40 * count * width, bytes_accessed=18 * count * width, transcendentals=0
        ),
    )(mine, got, middle, target, valid, gain, bias)


class Chain:
    def __init__(self):
        self.last = ()

    def step(self, *values):
        if self.last:
            values = lax.optimization_barrier(tuple(values) + self.last)[: len(values)]
        return values[0] if len(values) == 1 else tuple(values)

    def mark(self, *values):
        self.last = values
        return values[0] if len(values) == 1 else values


def relative_map(members, width):
    bits = members.bit_length() - 1
    block = width // members
    half = block // 2
    rel = jnp.arange(width)
    place = rel // half
    mask = jnp.zeros_like(rel)
    for k, bit in enumerate(range(bits - 1, 1, -1)):
        mask = mask | (((place >> k) & 1) << bit)
    side = (place >> (bits - 2)) & 1
    mask = mask | ((place >> (bits - 1)) & 3)
    source = (lax.axis_index("dp") ^ mask) * block + side * half + rel % half
    return (jnp.arange(width)[:, None] == source[None, :]).astype(jnp.bfloat16)


def high_bits():
    return tuple(range(lax.axis_size("dp").bit_length() - 2, 1, -1))


def as_halves(part):
    return part.reshape(2, part.shape[0] // 2, part.shape[1])


def as_rows(part):
    return part.reshape(-1, part.shape[-1])


def join_rows(*pieces):
    return lax.optimization_barrier(jnp.concatenate(pieces, axis=0))


def columns(left, *which):
    step = left.shape[1] // 8
    parts = [left[:, k * step : (k + 1) * step] for k in which]
    return parts[0] if len(parts) == 1 else jnp.concatenate(parts, axis=1)


def quarter(left, k):
    step = left.shape[1] // 4
    return left[:, k * step : (k + 1) * step]


def product_t(left, right):
    return low(
        lax.dot_general(left, right, (((0,), (0,)), ((), ())), preferred_element_type=jnp.float32)
    )


def collect_rows(values):
    if lax.axis_size("tensor") != 2:
        return lax.all_gather(values, "tensor", axis=0, tiled=True)
    return jnp.concatenate([values, swap_core(values)], axis=0)


def product_reduce(inputs, weight, dims, first=None):
    def product(rows):
        if first is not None:
            return matmul_t(rows, weight, first)
        return low(lax.dot_general(rows, weight, dims, preferred_element_type=jnp.float32))

    if lax.axis_size("tensor") != 2:
        return (
            lax.psum_scatter(product(inputs), "tensor", scatter_dimension=0, tiled=True),
            jnp.zeros((), jnp.bfloat16),
        )
    own_rows = inputs.shape[0] // 2
    got = swap_core(product(inputs[own_rows:]))
    return product(inputs[:own_rows]), got


def on_device(tokens, teacher, lengths, w_qkv, w_out, w_up, w_down, norm_gain, norm_bias):
    chain = Chain()
    step, mark = chain.step, chain.mark
    tok_dev, width = tokens.shape
    groups = lax.axis_size("tensor")
    members = lax.axis_size("dp")
    row_count = lengths.shape[0]
    group_tokens = tok_dev * groups
    slot_count = group_tokens // row_count
    all_slots = group_tokens * members
    me = lax.axis_index("tensor")
    own_places = me * tok_dev + jnp.arange(tok_dev)
    if groups == 2 and row_count == 1:
        places = jnp.concatenate([own_places, (1 - me) * tok_dev + jnp.arange(tok_dev)])
    else:
        places = jnp.arange(group_tokens)
    row_index = own_places // slot_count
    row_length = jnp.sum(
        jnp.where(row_index[:, None] == jnp.arange(row_count)[None, :], lengths[None, :], 0), axis=1
    )
    valid = (own_places % slot_count < row_length).astype(jnp.float32)[:, None]
    row_places = (places % slot_count).reshape(row_count, slot_count)
    angles = row_places[0].astype(jnp.float32)[:, None] * (
        10000.0 ** (-2.0 * jnp.arange(HEAD_DIM // 2).astype(jnp.float32) / HEAD_DIM)
    )
    cosine, sine = jnp.cos(angles)[:, None, :], jnp.sin(angles)[:, None, :]
    local_width = w_qkv.shape[2]
    heads_here = local_width // HEAD_DIM
    out_width = w_out.shape[1]
    hidden_width = w_up.shape[1]
    bits = high_bits()
    across = (((1,), (1,)), ((), ()))

    first_bits, last_bit = bits[:-1], bits[-1]

    def gather_first_z(part):
        for bit in first_bits:
            got = swap(part, bit)
            part = mark(jnp.concatenate(step(part, got), axis=1))
        return part

    def gather_last_z(part, got):
        return mark(jnp.concatenate(step(part, got), axis=1))

    def cut_z(terms):
        cut = terms[0].shape[1] // 2
        away = low(add_low(*[t[:, cut:] for t in terms]))
        return away, [t[:, :cut] for t in terms]

    def add_all_z(away, kept):
        terms = kept + [swap(away, last_bit)]
        for bit in first_bits[::-1]:
            away, kept = cut_z(list(step(*terms)))
            mark(away)
            terms = kept + [swap(away, bit)]
        return terms

    to_rel = relative_map(members, width)

    def relative(values):
        return jnp.dot(values, to_rel, preferred_element_type=jnp.float32)

    def absolute(values, precision=None):
        return lax.dot_general(
            values,
            to_rel.astype(values.dtype),
            (((1,), (1,)), ((), ())),
            precision=precision,
            preferred_element_type=jnp.float32,
        )

    def both(mine, got):
        return jnp.concatenate([mine, got], axis=0)

    def swap_rows(values):
        if groups == 2:
            return values, swap_core(values)
        every = lax.all_gather(values, "tensor", axis=0, tiled=True)
        return every, every[:0]

    one = as_halves(w_qkv.reshape(w_qkv.shape[0], 3 * local_width))
    two = as_halves(jnp.concatenate([w_out, w_up], axis=1))
    three_a, three_b = as_halves(w_down)
    three_got = swap(three_a, 0), swap(three_b, 1)
    one = gather_first_z(one)
    one_got = swap(one, last_bit)
    tokens, teacher, norm_gain, norm_bias = step(tokens, teacher, norm_gain, norm_bias)
    inputs = relative(tokens)
    target = low(relative(teacher))
    affine = jnp.dot(
        jnp.concatenate([norm_gain, norm_bias], axis=0),
        to_rel.astype(jnp.float32),
        precision=lax.Precision.HIGHEST,
        preferred_element_type=jnp.float32,
    )
    gain, bias = affine[:4], affine[4:]
    normal_zero, inv_zero = norm_stats(inputs)
    rows_one, other_one = swap_rows(mark(low(normal_zero * gain[0] + bias[0])))
    one = as_rows(gather_last_z(one, one_got))
    one_x, one_y = swap(one, 0), swap(one, 1)
    two = step(two)
    for bit in first_bits[:1]:
        two_got = swap(two, bit)
    three_a, three_b, three_xa, three_yb = step(three_a, three_b, *three_got)
    three = mark(jnp.stack([three_a, three_xa, three_b, three_yb], axis=0))
    two = mark(jnp.concatenate(step(two, two_got), axis=1))
    for bit in first_bits[1:]:
        two = mark(jnp.concatenate(step(two, swap(two, bit)), axis=1))
    two_got = swap(two, last_bit)
    three_got = swap(step(three), first_bits[0])
    cut = one.shape[0] // 2
    one_x, one_y = step(one_x, one_y)
    corner_a, corner_b = mark(one_x[:cut], one_y[cut:])
    corner_a, corner_b = swap(corner_a, 1), swap(corner_b, 0)
    two, two_got, corner_a, corner_b = step(two, two_got, corner_a, corner_b)
    two = mark(as_rows(jnp.concatenate([two, two_got], axis=1)))
    two_x, two_y = swap(two, 0), swap(two, 1)
    one, other_one = step(one, other_one)
    weight_qkv = join_rows(one, one_x, one_y, corner_a, corner_b)
    rows_one = both(rows_one, other_one)
    mixed = jnp.dot(rows_one, weight_qkv, preferred_element_type=jnp.float32)
    mixed = mixed.reshape(row_count, slot_count, 3, heads_here, HEAD_DIM)
    queries = low(rotate_pairs(mixed[:, :, 0], cosine, sine))
    key_rows = low(rotate_pairs(mixed[:, :, 1], cosine, sine))
    value_rows = low(mixed[:, :, 2])
    attended, totals = lax.map(
        attend_forward, (queries, key_rows, value_rows, lengths, row_places)
    )
    attended_low = mark(low(attended.reshape(group_tokens, local_width)))
    three = mark(jnp.concatenate(step(three, three_got), axis=1))
    for bit in first_bits[1:]:
        three = mark(jnp.concatenate(step(three, swap(three, bit)), axis=1))
    three_got = swap(three, last_bit)
    two_x, two_y = step(two_x, two_y)
    corner_a, corner_b = mark(two_x[:cut], two_y[cut:])
    corner_a, corner_b = swap(corner_a, 1), swap(corner_b, 0)
    three = gather_last_z(three, three_got)
    last_a, last_b = swap(three[:2], 1), swap(three[2:], 0)
    two, corner_a, corner_b = step(two, corner_a, corner_b)
    weight_mid = mark(join_rows(two, two_x, two_y, corner_a, corner_b))
    weight_out, weight_up = weight_mid[:, :out_width], weight_mid[:, out_width:]
    attn_mine, attn_got = product_reduce(attended_low, weight_out, across)
    mark(attn_mine)
    attn_sum = add_low(*step(attn_mine, attn_got))
    normal_one, inv_one = norm_stats(attn_sum)
    middle = inputs + normal_one * gain[1] + bias[1]
    normal_two, inv_two = norm_stats(middle)
    rows_two, other_two = swap_rows(mark(low(normal_two * gain[2] + bias[2])))
    rows_two = both(*step(rows_two, other_two))
    hidden = jnp.dot(rows_two, weight_up, preferred_element_type=jnp.float32)
    half = 0.5 * (1.0 + lax.erf(hidden * (2.0**-0.5)))
    active = low(hidden * half)
    slope = low(half + hidden * jnp.exp(-0.5 * hidden * hidden) * ((2.0 * jnp.pi) ** -0.5))
    active, slope = mark(*lax.optimization_barrier((active, slope)))
    (y_a0, y_a1), (x_b0, x_b1) = step(last_a, last_b)
    weight_down = mark(
        join_rows(three[0], three[2], three[1], x_b0, y_a0, three[3], y_a1, x_b1)
    )
    mine, got = product_reduce(active, weight_down, across)
    mark(mine)
    mine, got = step(mine, jnp.broadcast_to(got, mine.shape))
    result, out_grad, mlp_grad, last_sums = last_norm(
        mine, got, middle, target, valid, gain[3:4], bias[3:4]
    )
    mlp_rows, other = swap_rows(mark(mlp_grad))
    mlp_rows = both(*step(mlp_rows, other))

    def down_block(k):
        return mark(product_t(columns(step(mlp_rows), k), active))

    away = down_block(4), down_block(3)
    early = swap(away[0], 1), swap(away[1], 0)
    away = down_block(6), down_block(7)
    late = swap(away[0], 1), swap(away[1], 0)
    active_grad = jnp.dot(step(mlp_rows), weight_down, preferred_element_type=jnp.float32)
    hidden_grad = mark(low(active_grad * slope.astype(jnp.float32)))
    two_mine, two_got = product_reduce(hidden_grad, weight_mid, across, out_width)
    mark(two_mine)
    block = mark(product_t(quarter(step(rows_two), 3), hidden_grad))
    early = step(*early)
    corner_a, corner_b = swap(block[:cut], 1), swap(block[cut:], 0)
    kept = [down_block(k) for k in (0, 2, 1, 5)]
    normed_two_grad = add_low(*step(two_mine, two_got))
    middle_extra, gain_two, bias_two = norm_back(normed_two_grad, normal_two, inv_two, gain[2])
    middle_grad = out_grad + middle_extra
    attn_grad, gain_one, bias_one = norm_back(middle_grad, normal_one, inv_one, gain[1])
    attn_rows, other = swap_rows(mark(low(attn_grad)))
    blocks = [mark(product_t(quarter(step(rows_two), k), hidden_grad)) for k in (1, 2, 0)]
    late = step(*late)
    down = jnp.stack(
        [low(add_low(k, g)) for k, g in zip(kept, (early[0], late[0], early[1], late[1]))], axis=0
    )
    down_away, down_kept = cut_z([down])
    mark(down_away)
    down_got = swap(down_away, last_bit)
    attn_rows = both(*step(attn_rows, other))
    attended_grad = mark(
        low(jnp.dot(attn_rows, weight_out, preferred_element_type=jnp.float32))
    ).reshape(row_count, slot_count, heads_here, HEAD_DIM)

    def add_corners(over_x, over_y, from_y, from_x):
        over_x = jnp.concatenate([low(add_low(over_x[:cut], from_y)), over_x[cut:]], axis=0)
        over_y = jnp.concatenate([over_y[:cut], low(add_low(over_y[cut:], from_x))], axis=0)
        return mark(over_x, over_y)

    over_x, over_y = add_corners(*step(blocks[0], blocks[1], corner_a, corner_b))
    two_x, two_y = swap(over_x, 0), swap(over_y, 1)
    two_here = blocks[2]
    grads = [
        attend_backward(
            tuple(
                v[row]
                for v in (
                    queries, key_rows, value_rows, attended, attended_grad, totals, lengths,
                    row_places,
                )
            ),
            step,
            mark,
        )
        for row in range(row_count)
    ]
    query_grads, key_grads, value_grads = (jnp.stack(g, axis=0) for g in zip(*grads))
    query_grads, key_grads, value_grads = step(query_grads, key_grads, value_grads)
    mixed_grad = jnp.stack(
        [
            rotate_pairs(query_grads, cosine, -sine),
            rotate_pairs(key_grads, cosine, -sine),
            value_grads,
        ],
        axis=2,
    )
    mixed_grad = mark(low(mixed_grad.reshape(group_tokens, 3 * local_width)))

    def one_block(k):
        left, right = step(attn_rows, rows_one)
        return mark(
            jnp.concatenate(
                [
                    product_t(quarter(left, k), attended_low),
                    product_t(quarter(right, k), mixed_grad),
                ],
                axis=1,
            )
        )

    block = one_block(3)
    down_got, *down_kept = step(down_got, *down_kept)
    down_away, down_kept = cut_z(down_kept + [down_got])
    mark(down_away)
    for bit in first_bits[:0:-1]:
        down_away, down_kept = cut_z(down_kept + [step(swap(down_away, bit))])
        mark(down_away)
    down_got = swap(down_away, first_bits[0])
    two_here, two_x, two_y = step(two_here, two_x, two_y)
    corner_a, corner_b = swap(block[:cut], 1), swap(block[cut:], 0)
    two_away, two_kept = cut_z([as_halves(t) for t in (two_here, two_x, two_y)])
    mark(two_away)
    two_got = swap(two_away, last_bit)
    one_mine, one_got = product_reduce(step(mixed_grad), weight_qkv, across)
    mark(one_mine)
    blocks = [one_block(k) for k in (1, 2)]
    over_x, over_y = add_corners(*step(*blocks, corner_a, corner_b))
    one_x, one_y = swap(over_x, 0), swap(over_y, 1)
    one_here = one_block(0)
    normed_one_grad = add_low(*step(one_mine, one_got))
    input_extra, gain_zero, bias_zero = norm_back(normed_one_grad, normal_zero, inv_zero, gain[0])
    inputs_grad = mark(middle_grad + input_extra)
    last_sums = step(last_sums)
    gain_three, bias_three = jnp.sum(last_sums[:8], axis=0), jnp.sum(last_sums[8:16], axis=0)
    squared = jnp.sum(last_sums[16:])
    sums = jnp.stack(
        [
            gain_zero, gain_one, gain_two, gain_three,
            bias_zero, bias_one, bias_two, bias_three,
        ],
        axis=0,
    )
    total = jnp.concatenate(
        [jnp.broadcast_to(squared, (4, 128)), jnp.broadcast_to(jnp.sum(valid), (4, 128))], axis=0
    )
    if groups == 2:
        sums = mark(jnp.concatenate([step(sums), total], axis=1))
        total = swap_core(sums)
    else:
        sums = lax.psum(jnp.concatenate([sums, total], axis=1), "tensor")
        total = jnp.zeros_like(sums)

    def send_sums(sums, total, bit):
        middle_column = sums.shape[1] // 2
        sent = mark(jnp.concatenate([sums[:, middle_column:], total], axis=1))
        return sums[:, :middle_column], total, swap(sent, bit)

    def take_sums(sums, total, got):
        got = step(got)
        return sums + got[:, : sums.shape[1]], total + got[:, sums.shape[1] :]

    two_got, *two_kept = step(two_got, *two_kept)
    two_away, two_kept = cut_z(two_kept + [two_got])
    mark(two_away)
    for bit in first_bits[:0:-1]:
        two_away, two_kept = cut_z(two_kept + [step(swap(two_away, bit))])
        mark(two_away)
    two_got = swap(two_away, first_bits[0])
    down_got, *down_kept = step(down_got, *down_kept)
    down = add_low(*down_kept, down_got)
    down_low = mark(low(down))
    sums, total = step(sums, total)
    sums = sums + total
    pending = send_sums(sums[:, :width], sums[:, width:], 1)
    two_got, *two_kept = step(two_got, *two_kept)
    two = mark(low(add_low(*two_kept, two_got)))
    one_here, one_x, one_y = step(one_here, one_x, one_y)
    sums, total = take_sums(*pending)
    pending = send_sums(sums, total, 0)
    terms = [as_halves(t) for t in step(one_here, one_x, one_y)]
    one_away, one_kept = cut_z(terms)
    mark(one_away)
    sums, total = take_sums(*pending)
    middle_column = sums.shape[1] // 2
    sums = jnp.concatenate([sums[:, :middle_column], sums[:, middle_column:]], axis=0)
    total = jnp.concatenate([total, total], axis=0)
    for bit in reversed(bits):
        middle_column = sums.shape[1] // 2
        sent = jnp.concatenate([sums[:, middle_column:], total], axis=1)
        high = low(sent)
        sent = jnp.concatenate([high, low(sent - high.astype(jnp.float32))], axis=1)
        sent = jnp.pad(sent, ((0, 0), (0, one_away.shape[2] - sent.shape[1])))
        got = swap(mark(jnp.concatenate([as_rows(one_away), sent], axis=0)), bit)
        if bit == last_bit:
            down_low = step(down_low)
            down_got = swap(down_low[1], 0), swap(down_low[3], 1)
            inputs_grad = step(inputs_grad)
            tokens_grad = mark(absolute(inputs_grad, lax.Precision.HIGHEST))
        elif bit == bits[0]:
            layer_output = mark(low(absolute(step(result))))
        got, *one_kept = step(got, *one_kept)
        rows = one_away.shape[0] * one_away.shape[1]
        one_got = got[:rows].reshape(one_away.shape)
        got = got[rows:].astype(jnp.float32)
        span = middle_column + total.shape[1]
        got = got[:, :span] + got[:, span : 2 * span]
        sums, total = sums[:, :middle_column] + got[:, :middle_column], total + got[:, middle_column:]
        if bit != bits[0]:
            one_away, one_kept = cut_z(one_kept + [one_got])
    sums = jnp.concatenate([sums[:8], sums[8:]], axis=1)
    count = total[4, 0]
    scale = all_slots / count
    loss = total[0, 0] / (count * width)
    own = sums.shape[1] // groups
    sums = mark(lax.dynamic_slice_in_dim(sums, me * own, own, 1) * scale)
    two = as_rows(two.astype(jnp.float32) * scale)
    got_a, got_b = step(*down_got)
    down_part = mark(
        jnp.concatenate(
            [add_low(down[0], got_a) * scale, add_low(down[2], got_b) * scale], axis=0
        )
    )
    qkv_one = as_rows(add_low(*one_kept, one_got) * scale)
    return (
        loss,
        layer_output,
        tokens_grad * scale,
        qkv_one[:, out_width:].reshape(w_qkv.shape),
        qkv_one[:, :out_width],
        two,
        down_part,
        sums[:4],
        sums[4:],
    )


def solution(mesh):
    return jax.shard_map(
        on_device,
        mesh=mesh,
        in_specs=(
            P(("dp", "tensor"), None),
            P(("dp", "tensor"), None),
            P("dp"),
            P("dp", None, "tensor"),
            P("dp", "tensor"),
            P("dp", "tensor"),
            P("dp", "tensor"),
            P(),
            P(),
        ),
        out_specs=(
            P(),
            P(("dp", "tensor"), None),
            P(("dp", "tensor"), None),
            P("dp", None, "tensor"),
            P("dp", "tensor"),
            P("dp", "tensor"),
            P("dp", "tensor"),
            P(None, ("dp", "tensor")),
            P(None, ("dp", "tensor")),
        ),
        check_vma=False,
    )
```

```python
import jax
import jax.numpy as jnp
from jax import lax
from jax.experimental import pallas as pl
from jax.experimental.pallas import tpu as pltpu
from jax.sharding import PartitionSpec as P

HEAD_DIM = 64


norm_eps = 1e-05


def norm_stats(values):
    center = values - jnp.mean(values, axis=-1, keepdims=True)
    spread = jnp.mean(center * center, axis=-1, keepdims=True)
    inv = lax.rsqrt(spread + norm_eps)
    return center * inv, inv


def norm_back(grad, normal, inv, gain):
    e = grad * gain
    back = inv * (
        e
        - jnp.mean(e, axis=-1, keepdims=True)
        - normal * jnp.mean(e * normal, axis=-1, keepdims=True)
    )
    return back, jnp.sum(grad * normal, axis=0), jnp.sum(grad, axis=0)


def rotate_pairs(values, cosine, sine):
    half_size = values.shape[-1] // 2
    front = values[..., :half_size]
    back_half = values[..., half_size:]
    return jnp.concatenate(
        [front * cosine - back_half * sine, back_half * cosine + front * sine], axis=-1
    )


def attend_forward(packed):
    queries, key_rows, value_rows, length, places = packed
    slot_count = queries.shape[0]
    block = min(512, slot_count)
    scale = HEAD_DIM ** (-0.5)
    outputs = []
    totals = []
    for begin in range(0, slot_count, block):
        finish = begin + block
        scores = (
            jnp.einsum(
                "qhd,khd->hqk",
                queries[begin:finish],
                key_rows,
                preferred_element_type=jnp.float32,
            )
            * scale
        )
        allowed = (places[None, :] <= places[begin:finish, None]) & (places[None, :] < length)
        scores = jnp.where(allowed[None], scores, -1000000000.0)
        top_score = jnp.max(scores, axis=-1, keepdims=True)
        weights = jnp.exp(scores - top_score)
        weight_sum = jnp.sum(weights, axis=-1, keepdims=True)
        probs = (weights / weight_sum).astype(jnp.bfloat16)
        outputs.append(
            jnp.einsum("hqk,khd->qhd", probs, value_rows, preferred_element_type=jnp.float32)
        )
        totals.append((top_score + jnp.log(weight_sum))[:, :, 0])
    return (jnp.concatenate(outputs, axis=0), jnp.concatenate(totals, axis=1))


def attend_probs(packed):
    queries, key_rows, totals, length, places = packed
    slot_count = queries.shape[0]
    block = min(512, slot_count)
    probs = []
    for begin in range(0, slot_count, block):
        finish = begin + block
        scores = jnp.einsum(
            "qhd,khd->hqk", queries[begin:finish], key_rows, preferred_element_type=jnp.float32
        ) * HEAD_DIM ** (-0.5)
        allowed = (places[None, :] <= places[begin:finish, None]) & (places[None, :] < length)
        weights = jnp.exp(scores - totals[:, begin:finish, None])
        probs.append(low(jnp.where(allowed[None], weights, 0.0)))
    return probs


def attend_backward(packed, probs_low, step, mark):
    queries, key_rows, value_rows, outputs, out_grads = packed
    slot_count = queries.shape[0]
    block = min(512, slot_count)
    scale = HEAD_DIM ** (-0.5)
    delta = jnp.sum(out_grads.astype(jnp.float32) * outputs, axis=-1).T
    key_grads = 0.0
    value_grads = 0.0
    query_grads = []

    def product(form, left, right):
        left, right = step(left, right)
        return mark(jnp.einsum(form, left, right, preferred_element_type=jnp.float32))

    for begin in range(0, slot_count, block):
        finish = begin + block
        query_block = queries[begin:finish]
        grad_block = step(out_grads[begin:finish])
        probs = probs_low[begin // block]
        prob_grads = jnp.einsum(
            "qhd,khd->hqk", grad_block, value_rows, preferred_element_type=jnp.float32
        )
        score_grads = mark(
            low(probs.astype(jnp.float32) * (prob_grads - delta[:, begin:finish, None]))
        )
        value_grads = value_grads + product("hqk,qhd->khd", probs, grad_block)
        query_grads.append(product("hqk,khd->qhd", score_grads, key_rows) * scale)
        key_grads = key_grads + product("hqk,qhd->khd", score_grads, query_block) * scale
    return (jnp.concatenate(query_grads, axis=0), key_grads, value_grads)


def swap(values, bit):
    size = lax.axis_size("dp")
    return lax.ppermute(values, "dp", [(j, j ^ (1 << bit)) for j in range(size)])


def swap_core(values):
    return lax.ppermute(values, "tensor", [(0, 1), (1, 0)])


def add_low(*terms):
    total = terms[0].astype(jnp.float32)
    for term in terms[1:]:
        total = total + term.astype(jnp.float32)
    return total


def low(values):
    return values.astype(jnp.bfloat16)


def after(values, *others):
    return lax.optimization_barrier((values,) + others)[0]


def matmul_t(rows, weight, first, tile=256):
    count, depth = rows.shape
    outs = weight.shape[0]

    def kernel(rows_ref, weight_ref, out_ref):
        out_ref[...] = low(
            lax.dot_general(
                rows_ref[...],
                weight_ref[:, first : first + depth],
                (((1,), (1,)), ((), ())),
                preferred_element_type=jnp.float32,
            )
        )

    return pl.pallas_call(
        kernel,
        grid=(outs // tile,),
        in_specs=[
            pl.BlockSpec((count, depth), lambda j: (0, 0)),
            pl.BlockSpec((tile, weight.shape[1]), lambda j: (j, 0)),
        ],
        out_specs=pl.BlockSpec((count, tile), lambda j: (0, j)),
        out_shape=jax.ShapeDtypeStruct((count, outs), jnp.bfloat16),
        compiler_params=pltpu.CompilerParams(vmem_limit_bytes=16 * 1024 * 1024),
        cost_estimate=pl.CostEstimate(
            flops=2 * count * depth * outs, bytes_accessed=2 * outs * depth, transcendentals=0
        ),
    )(rows, weight)


def last_norm(mine, got, middle, target, valid, gain, bias):
    count, width = middle.shape
    chunk = 16
    share = 1.0 / width

    def kernel(mine_ref, got_ref, middle_ref, target_ref, valid_ref, gain_ref, bias_ref, *outs):
        result_ref, grad_ref, back_ref, sums_ref = outs
        sums_ref[...] = jnp.zeros_like(sums_ref)
        gains = gain_ref[...]

        def body(i, carry):
            rows = pl.ds(pl.multiple_of(i * chunk, chunk), chunk)
            values = add_low(mine_ref[rows, :], got_ref[rows, :])
            center = values - jnp.sum(values, axis=-1, keepdims=True) * share
            spread = jnp.sum(center * center, axis=-1, keepdims=True) * share
            inv = lax.rsqrt(spread + norm_eps)
            normal = center * inv
            result = middle_ref[rows, :] + normal * gains + bias_ref[...]
            result_ref[rows, :] = low(result)
            error = result - target_ref[rows, :].astype(jnp.float32)
            grad = valid_ref[rows, :] * error
            grad_ref[rows, :] = grad
            e = grad * gains
            turned = grad * normal
            mean_one = jnp.sum(e, axis=-1, keepdims=True) * share
            mean_two = jnp.sum(turned * gains, axis=-1, keepdims=True) * share
            back_ref[rows, :] = low(inv * (e - mean_one - normal * mean_two))
            for k, term in enumerate((turned, grad, grad * error)):
                sums_ref[8 * k : 8 * k + 8, :] += term[:8] + term[8:]
            return carry

        lax.fori_loop(0, count // chunk, body, 0, unroll=4)

    return pl.pallas_call(
        kernel,
        in_specs=[pl.BlockSpec(memory_space=pltpu.VMEM)] * 7,
        out_specs=[pl.BlockSpec(memory_space=pltpu.VMEM)] * 4,
        out_shape=[
            jax.ShapeDtypeStruct((count, width), jnp.bfloat16),
            jax.ShapeDtypeStruct((count, width), jnp.float32),
            jax.ShapeDtypeStruct((count, width), jnp.bfloat16),
            jax.ShapeDtypeStruct((24, width), jnp.float32),
        ],
        compiler_params=pltpu.CompilerParams(vmem_limit_bytes=8 * 1024 * 1024),
        cost_estimate=pl.CostEstimate(
            flops=40 * count * width, bytes_accessed=18 * count * width, transcendentals=0
        ),
    )(mine, got, middle, target, valid, gain, bias)


class Chain:
    def __init__(self):
        self.last = ()

    def step(self, *values):
        if self.last:
            values = lax.optimization_barrier(tuple(values) + self.last)[: len(values)]
        return values[0] if len(values) == 1 else tuple(values)

    def mark(self, *values):
        self.last = values
        return values[0] if len(values) == 1 else values


def relative_map(members, width):
    bits = members.bit_length() - 1
    block = width // members
    half = block // 2
    rel = jnp.arange(width)
    place = rel // half
    mask = jnp.zeros_like(rel)
    for k, bit in enumerate(range(bits - 1, 1, -1)):
        mask = mask | (((place >> k) & 1) << bit)
    side = (place >> (bits - 2)) & 1
    mask = mask | ((place >> (bits - 1)) & 3)
    source = (lax.axis_index("dp") ^ mask) * block + side * half + rel % half
    return (jnp.arange(width)[:, None] == source[None, :]).astype(jnp.bfloat16)


def high_bits():
    return tuple(range(lax.axis_size("dp").bit_length() - 2, 1, -1))


def as_halves(part):
    return part.reshape(2, part.shape[0] // 2, part.shape[1])


def as_rows(part):
    return part.reshape(-1, part.shape[-1])


def join_rows(*pieces):
    return lax.optimization_barrier(jnp.concatenate(pieces, axis=0))


def columns(left, *which):
    step = left.shape[1] // 8
    parts = [left[:, k * step : (k + 1) * step] for k in which]
    return parts[0] if len(parts) == 1 else jnp.concatenate(parts, axis=1)


def quarter(left, k):
    step = left.shape[1] // 4
    return left[:, k * step : (k + 1) * step]


def product_t(left, right):
    return low(
        lax.dot_general(left, right, (((0,), (0,)), ((), ())), preferred_element_type=jnp.float32)
    )


def collect_rows(values):
    if lax.axis_size("tensor") != 2:
        return lax.all_gather(values, "tensor", axis=0, tiled=True)
    return jnp.concatenate([values, swap_core(values)], axis=0)


def product_reduce(inputs, weight, dims, first=None):
    def product(rows):
        if first is not None:
            return matmul_t(rows, weight, first)
        return low(lax.dot_general(rows, weight, dims, preferred_element_type=jnp.float32))

    if lax.axis_size("tensor") != 2:
        return (
            lax.psum_scatter(product(inputs), "tensor", scatter_dimension=0, tiled=True),
            jnp.zeros((), jnp.bfloat16),
        )
    own_rows = inputs.shape[0] // 2
    got = swap_core(product(inputs[own_rows:]))
    return product(inputs[:own_rows]), got


def on_device(tokens, teacher, lengths, w_qkv, w_out, w_up, w_down, norm_gain, norm_bias):
    chain = Chain()
    step, mark = chain.step, chain.mark
    tok_dev, width = tokens.shape
    groups = lax.axis_size("tensor")
    members = lax.axis_size("dp")
    row_count = lengths.shape[0]
    group_tokens = tok_dev * groups
    slot_count = group_tokens // row_count
    all_slots = group_tokens * members
    me = lax.axis_index("tensor")
    own_places = me * tok_dev + jnp.arange(tok_dev)
    if groups == 2 and row_count == 1:
        places = jnp.concatenate([own_places, (1 - me) * tok_dev + jnp.arange(tok_dev)])
    else:
        places = jnp.arange(group_tokens)
    row_index = own_places // slot_count
    row_length = jnp.sum(
        jnp.where(row_index[:, None] == jnp.arange(row_count)[None, :], lengths[None, :], 0), axis=1
    )
    valid = (own_places % slot_count < row_length).astype(jnp.float32)[:, None]
    row_places = (places % slot_count).reshape(row_count, slot_count)
    angles = row_places[0].astype(jnp.float32)[:, None] * (
        10000.0 ** (-2.0 * jnp.arange(HEAD_DIM // 2).astype(jnp.float32) / HEAD_DIM)
    )
    cosine, sine = jnp.cos(angles)[:, None, :], jnp.sin(angles)[:, None, :]
    local_width = w_qkv.shape[2]
    heads_here = local_width // HEAD_DIM
    out_width = w_out.shape[1]
    hidden_width = w_up.shape[1]
    bits = high_bits()
    across = (((1,), (1,)), ((), ()))

    first_bits, last_bit = bits[:-1], bits[-1]

    def gather_first_z(part):
        for bit in first_bits:
            got = swap(part, bit)
            part = mark(jnp.concatenate(step(part, got), axis=1))
        return part

    def gather_last_z(part, got):
        return mark(jnp.concatenate(step(part, got), axis=1))

    def cut_z(terms):
        cut = terms[0].shape[1] // 2
        away = low(add_low(*[t[:, cut:] for t in terms]))
        return away, [t[:, :cut] for t in terms]

    def add_all_z(away, kept):
        terms = kept + [swap(away, last_bit)]
        for bit in first_bits[::-1]:
            away, kept = cut_z(list(step(*terms)))
            mark(away)
            terms = kept + [swap(away, bit)]
        return terms

    to_rel = relative_map(members, width)

    def relative(values):
        return jnp.dot(values, to_rel, preferred_element_type=jnp.float32)

    def absolute(values, precision=None):
        return lax.dot_general(
            values,
            to_rel.astype(values.dtype),
            (((1,), (1,)), ((), ())),
            precision=precision,
            preferred_element_type=jnp.float32,
        )

    def both(mine, got):
        return jnp.concatenate([mine, got], axis=0)

    def swap_rows(values):
        if groups == 2:
            return values, swap_core(values)
        every = lax.all_gather(values, "tensor", axis=0, tiled=True)
        return every, every[:0]

    one = as_halves(w_qkv.reshape(w_qkv.shape[0], 3 * local_width))
    two = as_halves(jnp.concatenate([w_out, w_up], axis=1))
    three_a, three_b = as_halves(w_down)
    three_got = swap(three_a, 0), swap(three_b, 1)
    one_a, one_b = one[:1], one[1:]
    counted = [jnp.sum(lengths).astype(jnp.float32).reshape(1, 1)]
    to_count = list(range(members.bit_length() - 1))

    def count_more():
        total = counted[-1]
        if len(counted) > 1:
            total = mark(sum(step(*counted)))
        counted[:] = [total, swap(total, to_count.pop(0))] if to_count else [total]

    count_more()
    got_a, got_b = swap(one_a, first_bits[0]), swap(one_b, first_bits[0])
    one_a = mark(jnp.concatenate(step(one_a, got_a), axis=1))
    for bit in first_bits[1:]:
        one_a = mark(jnp.concatenate(step(one_a, swap(one_a, bit)), axis=1))
    got_a = swap(one_a, last_bit)
    count_more()
    one_b = mark(jnp.concatenate(step(one_b, got_b), axis=1))
    for bit in first_bits[1:]:
        one_b = mark(jnp.concatenate(step(one_b, swap(one_b, bit)), axis=1))
    got_b = swap(one_b, last_bit)
    count_more()
    tokens, teacher, norm_gain, norm_bias = step(tokens, teacher, norm_gain, norm_bias)
    inputs = relative(tokens)
    target = low(relative(teacher))
    affine = jnp.dot(
        jnp.concatenate([norm_gain, norm_bias], axis=0),
        to_rel.astype(jnp.float32),
        precision=lax.Precision.HIGHEST,
        preferred_element_type=jnp.float32,
    )
    gain, bias = affine[:4], affine[4:]
    normal_zero, inv_zero = norm_stats(inputs)
    rows_one, other_one = swap_rows(mark(low(normal_zero * gain[0] + bias[0])))
    one = step(one_a, got_a, one_b, got_b)
    one = mark(jnp.concatenate([as_rows(p) for p in one], axis=0))
    one_x, one_y = swap(one, 0), swap(one, 1)
    count_more()
    two = step(two)
    for bit in first_bits[:1]:
        two_got = swap(two, bit)
    three_a, three_b, three_xa, three_yb = step(three_a, three_b, *three_got)
    three = mark(jnp.stack([three_a, three_xa, three_b, three_yb], axis=0))
    two = mark(jnp.concatenate(step(two, two_got), axis=1))
    for bit in first_bits[1:]:
        two = mark(jnp.concatenate(step(two, swap(two, bit)), axis=1))
    two_got = swap(two, last_bit)
    three_got = swap(step(three), first_bits[0])
    cut = one.shape[0] // 2
    one_x, one_y = step(one_x, one_y)
    corner_a, corner_b = mark(one_x[:cut], one_y[cut:])
    corner_a, corner_b = swap(corner_a, 1), swap(corner_b, 0)
    two = mark(as_rows(jnp.concatenate(step(two, two_got), axis=1)))
    two_x, two_y = swap(two, 0), swap(two, 1)
    one, other_one, corner_a, corner_b = step(one, other_one, corner_a, corner_b)
    weight_qkv = join_rows(one, one_x, one_y, corner_a, corner_b)
    rows_one = both(rows_one, other_one)
    mixed = jnp.dot(rows_one, weight_qkv, preferred_element_type=jnp.float32)
    mixed = mixed.reshape(row_count, slot_count, 3, heads_here, HEAD_DIM)
    queries = low(rotate_pairs(mixed[:, :, 0], cosine, sine))
    key_rows = low(rotate_pairs(mixed[:, :, 1], cosine, sine))
    value_rows = low(mixed[:, :, 2])
    attended, totals = lax.map(
        attend_forward, (queries, key_rows, value_rows, lengths, row_places)
    )
    attended_low = mark(low(attended.reshape(group_tokens, local_width)))
    while len(counted) > 1:
        count_more()
    weight = valid * (all_slots / counted[0])
    three = mark(jnp.concatenate(step(three, three_got), axis=1))
    for bit in first_bits[1:]:
        three = mark(jnp.concatenate(step(three, swap(three, bit)), axis=1))
    three_got = swap(three, last_bit)
    two_x, two_y = step(two_x, two_y)
    corner_a, corner_b = mark(two_x[:cut], two_y[cut:])
    corner_a, corner_b = swap(corner_a, 1), swap(corner_b, 0)
    three = gather_last_z(three, three_got)
    last_a, last_b = swap(three[:2], 1), swap(three[2:], 0)
    two, corner_a, corner_b = step(two, corner_a, corner_b)
    weight_mid = mark(join_rows(two, two_x, two_y, corner_a, corner_b))
    weight_out, weight_up = weight_mid[:, :out_width], weight_mid[:, out_width:]
    attn_mine, attn_got = product_reduce(attended_low, weight_out, across)
    mark(attn_mine)
    attn_sum = add_low(*step(attn_mine, attn_got))
    normal_one, inv_one = norm_stats(attn_sum)
    middle = inputs + normal_one * gain[1] + bias[1]
    normal_two, inv_two = norm_stats(middle)
    rows_two, other_two = swap_rows(mark(low(normal_two * gain[2] + bias[2])))
    rows_two = both(*step(rows_two, other_two))
    hidden = jnp.dot(rows_two, weight_up, preferred_element_type=jnp.float32)
    half = 0.5 * (1.0 + lax.erf(hidden * (2.0**-0.5)))
    active = low(hidden * half)
    slope = low(half + hidden * jnp.exp(-0.5 * hidden * hidden) * ((2.0 * jnp.pi) ** -0.5))
    active, slope = mark(*lax.optimization_barrier((active, slope)))
    (y_a0, y_a1), (x_b0, x_b1) = step(last_a, last_b)
    weight_down = mark(
        join_rows(three[0], three[2], three[1], x_b0, y_a0, three[3], y_a1, x_b1)
    )
    mine, got = product_reduce(active, weight_down, across)
    mark(mine)
    mine, got = step(mine, jnp.broadcast_to(got, mine.shape))
    result, out_grad, mlp_grad, last_sums = last_norm(
        mine, got, middle, target, weight, gain[3:4], bias[3:4]
    )
    mlp_rows, other = swap_rows(mark(mlp_grad))
    mlp_rows = both(*step(mlp_rows, other))

    def down_block(k):
        return mark(product_t(columns(step(mlp_rows), k), active))

    away = down_block(4), down_block(3)
    early = swap(away[0], 1), swap(away[1], 0)
    away = down_block(6), down_block(7)
    late = swap(away[0], 1), swap(away[1], 0)
    active_grad = jnp.dot(step(mlp_rows), weight_down, preferred_element_type=jnp.float32)
    hidden_grad = mark(low(active_grad * slope.astype(jnp.float32)))
    two_mine, two_got = product_reduce(hidden_grad, weight_mid, across, out_width)
    mark(two_mine)
    block = mark(product_t(quarter(step(rows_two), 3), hidden_grad))
    early = step(*early)
    corner_a, corner_b = swap(block[:cut], 1), swap(block[cut:], 0)
    kept = [down_block(k) for k in (0, 2, 1, 5)]
    normed_two_grad = add_low(*step(two_mine, two_got))
    middle_extra, gain_two, bias_two = norm_back(normed_two_grad, normal_two, inv_two, gain[2])
    middle_grad = out_grad + middle_extra
    attn_grad, gain_one, bias_one = norm_back(middle_grad, normal_one, inv_one, gain[1])
    attn_rows, other = swap_rows(mark(low(attn_grad)))
    blocks = [mark(product_t(quarter(step(rows_two), k), hidden_grad)) for k in (1, 2, 0)]
    late = step(*late)
    down = jnp.stack(
        [low(add_low(k, g)) for k, g in zip(kept, (early[0], late[0], early[1], late[1]))], axis=0
    )
    down_away, down_kept = cut_z([down])
    mark(down_away)
    down_got = swap(down_away, last_bit)
    queries_now, totals_now = step(queries, totals)
    probs_low = [
        attend_probs(
            tuple(v[row] for v in (queries_now, key_rows, totals_now, lengths, row_places))
        )
        for row in range(row_count)
    ]
    mark(*[p for row in probs_low for p in row])
    attn_rows = both(*step(attn_rows, other))
    attended_grad = mark(
        low(jnp.dot(attn_rows, weight_out, preferred_element_type=jnp.float32))
    ).reshape(row_count, slot_count, heads_here, HEAD_DIM)

    def add_corners(over_x, over_y, from_y, from_x):
        over_x = jnp.concatenate([low(add_low(over_x[:cut], from_y)), over_x[cut:]], axis=0)
        over_y = jnp.concatenate([over_y[:cut], low(add_low(over_y[cut:], from_x))], axis=0)
        return mark(over_x, over_y)

    over_x, over_y = add_corners(*step(blocks[0], blocks[1], corner_a, corner_b))
    two_x, two_y = swap(over_x, 0), swap(over_y, 1)
    two_here = blocks[2]
    grads = [
        attend_backward(
            tuple(v[row] for v in (queries, key_rows, value_rows, attended, attended_grad)),
            probs_low[row],
            step,
            mark,
        )
        for row in range(row_count)
    ]
    query_grads, key_grads, value_grads = (jnp.stack(g, axis=0) for g in zip(*grads))
    query_grads, key_grads, value_grads = step(query_grads, key_grads, value_grads)
    mixed_grad = jnp.stack(
        [
            rotate_pairs(query_grads, cosine, -sine),
            rotate_pairs(key_grads, cosine, -sine),
            value_grads,
        ],
        axis=2,
    )
    mixed_grad = mark(low(mixed_grad.reshape(group_tokens, 3 * local_width)))

    def one_block(k):
        left, right = step(attn_rows, rows_one)
        return mark(
            jnp.concatenate(
                [
                    product_t(quarter(left, k), attended_low),
                    product_t(quarter(right, k), mixed_grad),
                ],
                axis=1,
            )
        )

    block = one_block(3)
    down_got, *down_kept = step(down_got, *down_kept)
    down_away, down_kept = cut_z(down_kept + [down_got])
    mark(down_away)
    for bit in first_bits[:0:-1]:
        down_away, down_kept = cut_z(down_kept + [step(swap(down_away, bit))])
        mark(down_away)
    down_got = swap(down_away, first_bits[0])
    two_here, two_x, two_y = step(two_here, two_x, two_y)
    corner_a, corner_b = swap(block[:cut], 1), swap(block[cut:], 0)
    two_away, two_kept = cut_z([as_halves(t) for t in (two_here, two_x, two_y)])
    mark(two_away)
    two_got = swap(two_away, last_bit)
    one_mine, one_got = product_reduce(step(mixed_grad), weight_qkv, across)
    mark(one_mine)
    blocks = [one_block(k) for k in (1, 2)]
    over_x, over_y = add_corners(*step(*blocks, corner_a, corner_b))
    one_x, one_y = swap(over_x, 0), swap(over_y, 1)
    one_here = one_block(0)
    normed_one_grad = add_low(*step(one_mine, one_got))
    input_extra, gain_zero, bias_zero = norm_back(normed_one_grad, normal_zero, inv_zero, gain[0])
    inputs_grad = mark(middle_grad + input_extra)
    last_sums = step(last_sums)
    gain_three, bias_three = jnp.sum(last_sums[:8], axis=0), jnp.sum(last_sums[8:16], axis=0)
    squared = jnp.sum(last_sums[16:])
    sums = jnp.stack(
        [
            gain_zero, gain_one, gain_two, gain_three,
            bias_zero, bias_one, bias_two, bias_three,
        ],
        axis=0,
    )
    total = jnp.broadcast_to(squared, (8, 128))
    if groups == 2:
        sums = mark(jnp.concatenate([step(sums), total], axis=1))
        total = swap_core(sums)
    else:
        sums = lax.psum(jnp.concatenate([sums, total], axis=1), "tensor")
        total = jnp.zeros_like(sums)

    def send_sums(sums, total, bit):
        middle_column = sums.shape[1] // 2
        sent = mark(jnp.concatenate([sums[:, middle_column:], total], axis=1))
        return sums[:, :middle_column], total, swap(sent, bit)

    def take_sums(sums, total, got):
        got = step(got)
        return sums + got[:, : sums.shape[1]], total + got[:, sums.shape[1] :]

    two_got, *two_kept = step(two_got, *two_kept)
    two_away, two_kept = cut_z(two_kept + [two_got])
    mark(two_away)
    for bit in first_bits[:0:-1]:
        two_away, two_kept = cut_z(two_kept + [step(swap(two_away, bit))])
        mark(two_away)
    two_got = swap(two_away, first_bits[0])
    down_got, *down_kept = step(down_got, *down_kept)
    down = add_low(*down_kept, down_got)
    down_low = mark(low(down))
    sums, total = step(sums, total)
    sums = sums + total
    pending = send_sums(sums[:, :width], sums[:, width:], 1)
    two_got, *two_kept = step(two_got, *two_kept)
    two = mark(as_rows(add_low(*two_kept, two_got)))
    one_here, one_x, one_y = step(one_here, one_x, one_y)
    sums, total = take_sums(*pending)
    pending = send_sums(sums, total, 0)
    terms = [as_halves(t) for t in step(one_here, one_x, one_y)]
    one_away, one_kept = cut_z(terms)
    mark(one_away)
    sums, total = take_sums(*pending)
    middle_column = sums.shape[1] // 2
    sums = jnp.concatenate([sums[:, :middle_column], sums[:, middle_column:]], axis=0)
    total = jnp.concatenate([total, total], axis=0)

    def with_sums(away):
        sent = jnp.concatenate([sums[:, sums.shape[1] // 2 :], total], axis=1)
        high = low(sent)
        sent = jnp.concatenate([high, low(sent - high.astype(jnp.float32))], axis=1)
        sent = jnp.pad(sent, ((0, 0), (0, away.shape[2] - sent.shape[1])))
        return mark(jnp.concatenate([as_rows(away), sent], axis=0))

    def take_both(got, rows):
        middle_column = sums.shape[1] // 2
        span = middle_column + total.shape[1]
        extra = got[rows:].astype(jnp.float32)
        extra = extra[:, :span] + extra[:, span : 2 * span]
        return (
            got[:rows][None],
            sums[:, :middle_column] + extra[:, :middle_column],
            total + extra[:, middle_column:],
        )

    away_a, away_b = one_away[:1], one_away[1:]
    one_kept = mark(low(add_low(*one_kept)))
    kept_a, kept_b = [one_kept[:1]], [one_kept[1:]]
    got_a = swap(with_sums(away_a), last_bit)
    got_b = swap(mark(step(away_b)), last_bit)
    down_low = step(down_low)
    down_got = swap(down_low[1], 0), swap(down_low[3], 1)
    inputs_grad = step(inputs_grad)
    tokens_grad = mark(absolute(inputs_grad, lax.Precision.HIGHEST))
    for bit in first_bits[::-1]:
        got_a, *kept_a = step(got_a, *kept_a)
        got_a, sums, total = take_both(got_a, away_a.shape[1])
        away_a, kept_a = cut_z(kept_a + [got_a])
        got_a = swap(with_sums(away_a), bit)
        got_b, *kept_b = step(got_b, *kept_b)
        away_b, kept_b = cut_z(kept_b + [got_b])
        got_b = swap(mark(away_b), bit)
    layer_output = mark(low(absolute(step(result))))
    down_a, down_b = step(*down_got)
    down_part = mark(jnp.concatenate([add_low(down[0], down_a), add_low(down[2], down_b)], axis=0))
    got_a, *kept_a = step(got_a, *kept_a)
    got_a, sums, total = take_both(got_a, away_a.shape[1])
    got_b, *kept_b = step(got_b, *kept_b)
    sums = jnp.concatenate([sums[:8], sums[8:]], axis=1)
    loss = total[0, 0] / (all_slots * width)
    own = sums.shape[1] // groups
    sums = lax.dynamic_slice_in_dim(sums, me * own, own, 1)
    one = jnp.concatenate([add_low(*kept_a, got_a), add_low(*kept_b, got_b)], axis=0)
    qkv_one = as_rows(one)
    return (
        loss,
        layer_output,
        tokens_grad,
        qkv_one[:, out_width:].reshape(w_qkv.shape),
        qkv_one[:, :out_width],
        two,
        down_part,
        sums[:4],
        sums[4:],
    )


def solution(mesh):
    return jax.shard_map(
        on_device,
        mesh=mesh,
        in_specs=(
            P(("dp", "tensor"), None),
            P(("dp", "tensor"), None),
            P("dp"),
            P("dp", None, "tensor"),
            P("dp", "tensor"),
            P("dp", "tensor"),
            P("dp", "tensor"),
            P(),
            P(),
        ),
        out_specs=(
            P(),
            P(("dp", "tensor"), None),
            P(("dp", "tensor"), None),
            P("dp", None, "tensor"),
            P("dp", "tensor"),
            P("dp", "tensor"),
            P("dp", "tensor"),
            P(None, ("dp", "tensor")),
            P(None, ("dp", "tensor")),
        ),
        check_vma=False,
    )
```

```python
import jax
import jax.numpy as jnp
from jax import lax
from jax.experimental import pallas as pl
from jax.experimental.pallas import tpu as pltpu
from jax.sharding import PartitionSpec as P

HEAD_DIM = 64


norm_eps = 1e-05


def norm_stats(values):
    center = values - jnp.mean(values, axis=-1, keepdims=True)
    spread = jnp.mean(center * center, axis=-1, keepdims=True)
    inv = lax.rsqrt(spread + norm_eps)
    return center * inv, inv


def norm_back(grad, normal, inv, gain):
    e = grad * gain
    back = inv * (
        e
        - jnp.mean(e, axis=-1, keepdims=True)
        - normal * jnp.mean(e * normal, axis=-1, keepdims=True)
    )
    return back, jnp.sum(grad * normal, axis=0), jnp.sum(grad, axis=0)


def rotate_pairs(values, cosine, sine):
    half_size = values.shape[-1] // 2
    front = values[..., :half_size]
    back_half = values[..., half_size:]
    return jnp.concatenate(
        [front * cosine - back_half * sine, back_half * cosine + front * sine], axis=-1
    )


def attend_forward(packed):
    queries, key_rows, value_rows, length, places = packed
    slot_count = queries.shape[0]
    block = min(512, slot_count)
    scale = HEAD_DIM ** (-0.5)
    outputs = []
    totals = []
    for begin in range(0, slot_count, block):
        finish = begin + block
        scores = (
            jnp.einsum(
                "qhd,khd->hqk",
                queries[begin:finish],
                key_rows,
                preferred_element_type=jnp.float32,
            )
            * scale
        )
        allowed = (places[None, :] <= places[begin:finish, None]) & (places[None, :] < length)
        scores = jnp.where(allowed[None], scores, -1000000000.0)
        top_score = jnp.max(scores, axis=-1, keepdims=True)
        weights = jnp.exp(scores - top_score)
        weight_sum = jnp.sum(weights, axis=-1, keepdims=True)
        probs = (weights / weight_sum).astype(jnp.bfloat16)
        outputs.append(
            jnp.einsum("hqk,khd->qhd", probs, value_rows, preferred_element_type=jnp.float32)
        )
        totals.append((top_score + jnp.log(weight_sum))[:, :, 0])
    return (jnp.concatenate(outputs, axis=0), jnp.concatenate(totals, axis=1))


def attend_probs(packed):
    queries, key_rows, totals, length, places = packed
    slot_count = queries.shape[0]
    block = min(512, slot_count)
    probs = []
    for begin in range(0, slot_count, block):
        finish = begin + block
        scores = jnp.einsum(
            "qhd,khd->hqk", queries[begin:finish], key_rows, preferred_element_type=jnp.float32
        ) * HEAD_DIM ** (-0.5)
        allowed = (places[None, :] <= places[begin:finish, None]) & (places[None, :] < length)
        weights = jnp.exp(scores - totals[:, begin:finish, None])
        probs.append(low(jnp.where(allowed[None], weights, 0.0)))
    return probs


def attend_backward(packed, probs_low, step, mark):
    queries, key_rows, value_rows, outputs, out_grads = packed
    slot_count = queries.shape[0]
    block = min(512, slot_count)
    scale = HEAD_DIM ** (-0.5)
    delta = jnp.sum(out_grads.astype(jnp.float32) * outputs, axis=-1).T
    key_grads = 0.0
    value_grads = 0.0
    query_grads = []

    def product(form, left, right):
        left, right = step(left, right)
        return mark(jnp.einsum(form, left, right, preferred_element_type=jnp.float32))

    for begin in range(0, slot_count, block):
        finish = begin + block
        query_block = queries[begin:finish]
        grad_block = step(out_grads[begin:finish])
        probs = probs_low[begin // block]
        prob_grads = jnp.einsum(
            "qhd,khd->hqk", grad_block, value_rows, preferred_element_type=jnp.float32
        )
        score_grads = mark(
            low(probs.astype(jnp.float32) * (prob_grads - delta[:, begin:finish, None]))
        )
        value_grads = value_grads + product("hqk,qhd->khd", probs, grad_block)
        query_grads.append(product("hqk,khd->qhd", score_grads, key_rows) * scale)
        key_grads = key_grads + product("hqk,qhd->khd", score_grads, query_block) * scale
    return (jnp.concatenate(query_grads, axis=0), key_grads, value_grads)


def swap(values, bit):
    size = lax.axis_size("dp")
    return lax.ppermute(values, "dp", [(j, j ^ (1 << bit)) for j in range(size)])


def swap_core(values):
    return lax.ppermute(values, "tensor", [(0, 1), (1, 0)])


def add_low(*terms):
    total = terms[0].astype(jnp.float32)
    for term in terms[1:]:
        total = total + term.astype(jnp.float32)
    return total


def low(values):
    return values.astype(jnp.bfloat16)


def after(values, *others):
    return lax.optimization_barrier((values,) + others)[0]


def matmul_t(rows, weight, first, tile=256):
    count, depth = rows.shape
    outs = weight.shape[0]

    def kernel(rows_ref, weight_ref, out_ref):
        out_ref[...] = low(
            lax.dot_general(
                rows_ref[...],
                weight_ref[:, first : first + depth],
                (((1,), (1,)), ((), ())),
                preferred_element_type=jnp.float32,
            )
        )

    return pl.pallas_call(
        kernel,
        grid=(outs // tile,),
        in_specs=[
            pl.BlockSpec((count, depth), lambda j: (0, 0)),
            pl.BlockSpec((tile, weight.shape[1]), lambda j: (j, 0)),
        ],
        out_specs=pl.BlockSpec((count, tile), lambda j: (0, j)),
        out_shape=jax.ShapeDtypeStruct((count, outs), jnp.bfloat16),
        compiler_params=pltpu.CompilerParams(vmem_limit_bytes=16 * 1024 * 1024),
        cost_estimate=pl.CostEstimate(
            flops=2 * count * depth * outs, bytes_accessed=2 * outs * depth, transcendentals=0
        ),
    )(rows, weight)


def last_norm(mine, got, middle, target, valid, gain, bias):
    count, width = middle.shape
    chunk = 16
    share = 1.0 / width

    def kernel(mine_ref, got_ref, middle_ref, target_ref, valid_ref, gain_ref, bias_ref, *outs):
        result_ref, grad_ref, back_ref, sums_ref = outs
        sums_ref[...] = jnp.zeros_like(sums_ref)
        gains = gain_ref[...]

        def body(i, carry):
            rows = pl.ds(pl.multiple_of(i * chunk, chunk), chunk)
            values = add_low(mine_ref[rows, :], got_ref[rows, :])
            center = values - jnp.sum(values, axis=-1, keepdims=True) * share
            spread = jnp.sum(center * center, axis=-1, keepdims=True) * share
            inv = lax.rsqrt(spread + norm_eps)
            normal = center * inv
            result = middle_ref[rows, :] + normal * gains + bias_ref[...]
            result_ref[rows, :] = low(result)
            error = result - target_ref[rows, :].astype(jnp.float32)
            grad = valid_ref[rows, :] * error
            grad_ref[rows, :] = grad
            e = grad * gains
            turned = grad * normal
            mean_one = jnp.sum(e, axis=-1, keepdims=True) * share
            mean_two = jnp.sum(turned * gains, axis=-1, keepdims=True) * share
            back_ref[rows, :] = low(inv * (e - mean_one - normal * mean_two))
            for k, term in enumerate((turned, grad, grad * error)):
                sums_ref[8 * k : 8 * k + 8, :] += term[:8] + term[8:]
            return carry

        lax.fori_loop(0, count // chunk, body, 0, unroll=4)

    return pl.pallas_call(
        kernel,
        in_specs=[pl.BlockSpec(memory_space=pltpu.VMEM)] * 7,
        out_specs=[pl.BlockSpec(memory_space=pltpu.VMEM)] * 4,
        out_shape=[
            jax.ShapeDtypeStruct((count, width), jnp.bfloat16),
            jax.ShapeDtypeStruct((count, width), jnp.float32),
            jax.ShapeDtypeStruct((count, width), jnp.bfloat16),
            jax.ShapeDtypeStruct((24, width), jnp.float32),
        ],
        compiler_params=pltpu.CompilerParams(vmem_limit_bytes=8 * 1024 * 1024),
        cost_estimate=pl.CostEstimate(
            flops=40 * count * width, bytes_accessed=18 * count * width, transcendentals=0
        ),
    )(mine, got, middle, target, valid, gain, bias)


class Chain:
    def __init__(self):
        self.last = ()

    def step(self, *values):
        if self.last:
            values = lax.optimization_barrier(tuple(values) + self.last)[: len(values)]
        return values[0] if len(values) == 1 else tuple(values)

    def mark(self, *values):
        self.last = values
        return values[0] if len(values) == 1 else values


def relative_map(members, width):
    bits = members.bit_length() - 1
    block = width // members
    half = block // 2
    rel = jnp.arange(width)
    place = rel // half
    mask = jnp.zeros_like(rel)
    for k, bit in enumerate(range(bits - 1, 1, -1)):
        mask = mask | (((place >> k) & 1) << bit)
    side = (place >> (bits - 2)) & 1
    mask = mask | ((place >> (bits - 1)) & 3)
    source = (lax.axis_index("dp") ^ mask) * block + side * half + rel % half
    return (jnp.arange(width)[:, None] == source[None, :]).astype(jnp.bfloat16)


def high_bits():
    return tuple(range(lax.axis_size("dp").bit_length() - 2, 1, -1))


def as_halves(part):
    return part.reshape(2, part.shape[0] // 2, part.shape[1])


def as_rows(part):
    return part.reshape(-1, part.shape[-1])


def join_rows(*pieces):
    return lax.optimization_barrier(jnp.concatenate(pieces, axis=0))


def columns(left, *which):
    step = left.shape[1] // 8
    parts = [left[:, k * step : (k + 1) * step] for k in which]
    return parts[0] if len(parts) == 1 else jnp.concatenate(parts, axis=1)


def quarter(left, k):
    step = left.shape[1] // 4
    return left[:, k * step : (k + 1) * step]


def product_t(left, right):
    return low(
        lax.dot_general(left, right, (((0,), (0,)), ((), ())), preferred_element_type=jnp.float32)
    )


def collect_rows(values):
    if lax.axis_size("tensor") != 2:
        return lax.all_gather(values, "tensor", axis=0, tiled=True)
    return jnp.concatenate([values, swap_core(values)], axis=0)


def product_reduce(inputs, weight, dims, first=None):
    def product(rows):
        if first is not None:
            return matmul_t(rows, weight, first)
        return low(lax.dot_general(rows, weight, dims, preferred_element_type=jnp.float32))

    if lax.axis_size("tensor") != 2:
        return (
            lax.psum_scatter(product(inputs), "tensor", scatter_dimension=0, tiled=True),
            jnp.zeros((), jnp.bfloat16),
        )
    own_rows = inputs.shape[0] // 2
    got = swap_core(product(inputs[own_rows:]))
    return product(inputs[:own_rows]), got


def on_device(tokens, teacher, lengths, w_qkv, w_out, w_up, w_down, norm_gain, norm_bias):
    chain = Chain()
    step, mark = chain.step, chain.mark
    tok_dev, width = tokens.shape
    groups = lax.axis_size("tensor")
    members = lax.axis_size("dp")
    row_count = lengths.shape[0]
    group_tokens = tok_dev * groups
    slot_count = group_tokens // row_count
    all_slots = group_tokens * members
    me = lax.axis_index("tensor")
    own_places = me * tok_dev + jnp.arange(tok_dev)
    if groups == 2 and row_count == 1:
        places = jnp.concatenate([own_places, (1 - me) * tok_dev + jnp.arange(tok_dev)])
    else:
        places = jnp.arange(group_tokens)
    row_index = own_places // slot_count
    row_length = jnp.sum(
        jnp.where(row_index[:, None] == jnp.arange(row_count)[None, :], lengths[None, :], 0), axis=1
    )
    valid = (own_places % slot_count < row_length).astype(jnp.float32)[:, None]
    row_places = (places % slot_count).reshape(row_count, slot_count)
    angles = row_places[0].astype(jnp.float32)[:, None] * (
        10000.0 ** (-2.0 * jnp.arange(HEAD_DIM // 2).astype(jnp.float32) / HEAD_DIM)
    )
    cosine, sine = jnp.cos(angles)[:, None, :], jnp.sin(angles)[:, None, :]
    local_width = w_qkv.shape[2]
    heads_here = local_width // HEAD_DIM
    out_width = w_out.shape[1]
    hidden_width = w_up.shape[1]
    bits = high_bits()
    across = (((1,), (1,)), ((), ()))

    first_bits, last_bit = bits[:-1], bits[-1]

    def gather_first_z(part):
        for bit in first_bits:
            got = swap(part, bit)
            part = mark(jnp.concatenate(step(part, got), axis=1))
        return part

    def gather_last_z(part, got):
        return mark(jnp.concatenate(step(part, got), axis=1))

    def cut_z(terms):
        cut = terms[0].shape[1] // 2
        away = low(add_low(*[t[:, cut:] for t in terms]))
        return away, [t[:, :cut] for t in terms]

    def add_all_z(away, kept):
        terms = kept + [swap(away, last_bit)]
        for bit in first_bits[::-1]:
            away, kept = cut_z(list(step(*terms)))
            mark(away)
            terms = kept + [swap(away, bit)]
        return terms

    to_rel = relative_map(members, width)

    def relative(values):
        return jnp.dot(values, to_rel, preferred_element_type=jnp.float32)

    def absolute(values, precision=None):
        return lax.dot_general(
            values,
            to_rel.astype(values.dtype),
            (((1,), (1,)), ((), ())),
            precision=precision,
            preferred_element_type=jnp.float32,
        )

    def both(mine, got):
        return jnp.concatenate([mine, got], axis=0)

    def swap_rows(values):
        if groups == 2:
            return values, swap_core(values)
        every = lax.all_gather(values, "tensor", axis=0, tiled=True)
        return every, every[:0]

    one = as_halves(w_qkv.reshape(w_qkv.shape[0], 3 * local_width))
    two = as_halves(jnp.concatenate([w_out, w_up], axis=1))
    three_a, three_b = as_halves(w_down)
    three_got = swap(three_a, 0), swap(three_b, 1)
    one_a, one_b = one[:1], one[1:]
    counted = [jnp.sum(lengths).astype(jnp.float32).reshape(1, 1)]
    to_count = [0, bits[0], 1, *bits[1:]]

    def count_more():
        total = counted[-1]
        if len(counted) > 1:
            total = mark(sum(step(*counted)))
        counted[:] = [total, swap(total, to_count.pop(0))] if to_count else [total]

    count_more()
    got_a, got_b = swap(one_a, first_bits[0]), swap(one_b, first_bits[0])
    one_a = mark(jnp.concatenate(step(one_a, got_a), axis=1))
    for bit in first_bits[1:]:
        one_a = mark(jnp.concatenate(step(one_a, swap(one_a, bit)), axis=1))
    got_a = swap(one_a, last_bit)
    count_more()
    one_b = mark(jnp.concatenate(step(one_b, got_b), axis=1))
    for bit in first_bits[1:]:
        one_b = mark(jnp.concatenate(step(one_b, swap(one_b, bit)), axis=1))
    got_b = swap(one_b, last_bit)
    count_more()
    tokens, teacher, norm_gain, norm_bias = step(tokens, teacher, norm_gain, norm_bias)
    inputs = relative(tokens)
    target = low(relative(teacher))
    affine = jnp.dot(
        jnp.concatenate([norm_gain, norm_bias], axis=0),
        to_rel.astype(jnp.float32),
        precision=lax.Precision.HIGHEST,
        preferred_element_type=jnp.float32,
    )
    gain, bias = affine[:4], affine[4:]
    normal_zero, inv_zero = norm_stats(inputs)
    rows_one, other_one = swap_rows(mark(low(normal_zero * gain[0] + bias[0])))
    one = step(one_a, got_a, one_b, got_b)
    one = mark(jnp.concatenate([as_rows(p) for p in one], axis=0))
    one_x, one_y = swap(one, 0), swap(one, 1)
    count_more()
    two = step(two)
    for bit in first_bits[:1]:
        two_got = swap(two, bit)
    three_a, three_b, three_xa, three_yb = step(three_a, three_b, *three_got)
    three = mark(jnp.stack([three_a, three_xa, three_b, three_yb], axis=0))
    two = mark(jnp.concatenate(step(two, two_got), axis=1))
    for bit in first_bits[1:]:
        two = mark(jnp.concatenate(step(two, swap(two, bit)), axis=1))
    two_got = swap(two, last_bit)
    three_got = swap(step(three), first_bits[0])
    cut = one.shape[0] // 2
    one_x, one_y = step(one_x, one_y)
    corner_a, corner_b = mark(one_x[:cut], one_y[cut:])
    corner_a, corner_b = swap(corner_a, 1), swap(corner_b, 0)
    two = mark(as_rows(jnp.concatenate(step(two, two_got), axis=1)))
    two_x, two_y = swap(two, 0), swap(two, 1)
    one, other_one, corner_a, corner_b = step(one, other_one, corner_a, corner_b)
    weight_qkv = join_rows(one, one_x, one_y, corner_a, corner_b)
    rows_one = both(rows_one, other_one)
    mixed = jnp.dot(rows_one, weight_qkv, preferred_element_type=jnp.float32)
    mixed = mixed.reshape(row_count, slot_count, 3, heads_here, HEAD_DIM)
    queries = low(rotate_pairs(mixed[:, :, 0], cosine, sine))
    key_rows = low(rotate_pairs(mixed[:, :, 1], cosine, sine))
    value_rows = low(mixed[:, :, 2])
    attended, totals = lax.map(
        attend_forward, (queries, key_rows, value_rows, lengths, row_places)
    )
    attended_low = mark(low(attended.reshape(group_tokens, local_width)))
    while len(counted) > 1:
        count_more()
    weight = valid * (all_slots / counted[0])
    three = mark(jnp.concatenate(step(three, three_got), axis=1))
    for bit in first_bits[1:]:
        three = mark(jnp.concatenate(step(three, swap(three, bit)), axis=1))
    three_got = swap(three, last_bit)
    two_x, two_y = step(two_x, two_y)
    corner_a, corner_b = mark(two_x[:cut], two_y[cut:])
    corner_a, corner_b = swap(corner_a, 1), swap(corner_b, 0)
    three = gather_last_z(three, three_got)
    last_a, last_b = swap(three[:2], 1), swap(three[2:], 0)
    two, corner_a, corner_b = step(two, corner_a, corner_b)
    weight_mid = mark(join_rows(two, two_x, two_y, corner_a, corner_b))
    weight_out, weight_up = weight_mid[:, :out_width], weight_mid[:, out_width:]
    attn_mine, attn_got = product_reduce(attended_low, weight_out, across)
    mark(attn_mine)
    attn_sum = add_low(*step(attn_mine, attn_got))
    normal_one, inv_one = norm_stats(attn_sum)
    middle = inputs + normal_one * gain[1] + bias[1]
    normal_two, inv_two = norm_stats(middle)
    rows_two, other_two = swap_rows(mark(low(normal_two * gain[2] + bias[2])))
    rows_two = both(*step(rows_two, other_two))
    hidden = jnp.dot(rows_two, weight_up, preferred_element_type=jnp.float32)
    half = 0.5 * (1.0 + lax.erf(hidden * (2.0**-0.5)))
    active = low(hidden * half)
    slope = low(half + hidden * jnp.exp(-0.5 * hidden * hidden) * ((2.0 * jnp.pi) ** -0.5))
    active, slope = mark(*lax.optimization_barrier((active, slope)))
    (y_a0, y_a1), (x_b0, x_b1) = step(last_a, last_b)
    weight_down = mark(
        join_rows(three[0], three[2], three[1], x_b0, y_a0, three[3], y_a1, x_b1)
    )
    mine, got = product_reduce(active, weight_down, across)
    mark(mine)
    mine, got = step(mine, jnp.broadcast_to(got, mine.shape))
    result, out_grad, mlp_grad, last_sums = last_norm(
        mine, got, middle, target, weight, gain[3:4], bias[3:4]
    )
    mlp_rows, other = swap_rows(mark(mlp_grad))
    mlp_rows = both(*step(mlp_rows, other))

    def down_block(k):
        return mark(product_t(columns(step(mlp_rows), k), active))

    away = down_block(4), down_block(3)
    early = swap(away[0], 1), swap(away[1], 0)
    away = down_block(6), down_block(7)
    late = swap(away[0], 1), swap(away[1], 0)
    active_grad = jnp.dot(step(mlp_rows), weight_down, preferred_element_type=jnp.float32)
    hidden_grad = mark(low(active_grad * slope.astype(jnp.float32)))
    two_mine, two_got = product_reduce(hidden_grad, weight_mid, across, out_width)
    mark(two_mine)
    block = mark(product_t(quarter(step(rows_two), 3), hidden_grad))
    early = step(*early)
    corner_a, corner_b = swap(block[:cut], 1), swap(block[cut:], 0)
    kept = [down_block(k) for k in (0, 2, 1, 5)]
    normed_two_grad = add_low(*step(two_mine, two_got))
    middle_extra, gain_two, bias_two = norm_back(normed_two_grad, normal_two, inv_two, gain[2])
    middle_grad = out_grad + middle_extra
    attn_grad, gain_one, bias_one = norm_back(middle_grad, normal_one, inv_one, gain[1])
    attn_rows, other = swap_rows(mark(low(attn_grad)))
    def up_block(k):
        return mark(product_t(columns(step(rows_two), k), hidden_grad))

    side_b, side_a = up_block(3), up_block(4)
    two_xb, two_ya = swap(side_b, 0), swap(side_a, 1)
    side_a, side_b = up_block(2), up_block(5)
    two_here = mark(product_t(quarter(step(rows_two), 0), hidden_grad))
    late = step(*late)
    down = jnp.stack(
        [low(add_low(k, g)) for k, g in zip(kept, (early[0], late[0], early[1], late[1]))], axis=0
    )
    down_away, down_kept = cut_z([down])
    mark(down_away)
    down_got = swap(down_away, last_bit)
    queries_now, totals_now = step(queries, totals)
    probs_low = [
        attend_probs(
            tuple(v[row] for v in (queries_now, key_rows, totals_now, lengths, row_places))
        )
        for row in range(row_count)
    ]
    mark(*[p for row in probs_low for p in row])
    attn_rows = both(*step(attn_rows, other))
    attended_grad = mark(
        low(jnp.dot(attn_rows, weight_out, preferred_element_type=jnp.float32))
    ).reshape(row_count, slot_count, heads_here, HEAD_DIM)

    side_a = mark(low(add_low(side_a, step(corner_a))))
    side_b = mark(low(add_low(side_b, step(corner_b))))
    two_xa, two_yb = swap(side_a, 0), swap(side_b, 1)
    grads = [
        attend_backward(
            tuple(v[row] for v in (queries, key_rows, value_rows, attended, attended_grad)),
            probs_low[row],
            step,
            mark,
        )
        for row in range(row_count)
    ]
    query_grads, key_grads, value_grads = (jnp.stack(g, axis=0) for g in zip(*grads))
    query_grads, key_grads, value_grads = step(query_grads, key_grads, value_grads)
    mixed_grad = jnp.stack(
        [
            rotate_pairs(query_grads, cosine, -sine),
            rotate_pairs(key_grads, cosine, -sine),
            value_grads,
        ],
        axis=2,
    )
    mixed_grad = mark(low(mixed_grad.reshape(group_tokens, 3 * local_width)))

    def add_corners(over_x, over_y, from_y, from_x):
        over_x = jnp.concatenate([low(add_low(over_x[:cut], from_y)), over_x[cut:]], axis=0)
        over_y = jnp.concatenate([over_y[:cut], low(add_low(over_y[cut:], from_x))], axis=0)
        return mark(over_x, over_y)

    def one_block(k):
        left, right = step(attn_rows, rows_one)
        return mark(
            jnp.concatenate(
                [
                    product_t(quarter(left, k), attended_low),
                    product_t(quarter(right, k), mixed_grad),
                ],
                axis=1,
            )
        )

    block = one_block(3)
    down_got, *down_kept = step(down_got, *down_kept)
    down_away, down_kept = cut_z(down_kept + [down_got])
    mark(down_away)
    for bit in first_bits[:0:-1]:
        down_away, down_kept = cut_z(down_kept + [step(swap(down_away, bit))])
        mark(down_away)
    down_got = swap(down_away, first_bits[0])
    two_xa, two_xb, two_ya, two_yb = step(two_xa, two_xb, two_ya, two_yb)
    corner_a, corner_b = swap(block[:cut], 1), swap(block[cut:], 0)
    two_away, two_kept = cut_z(
        [as_halves(two_here), jnp.stack([two_xa, two_xb]), jnp.stack([two_ya, two_yb])]
    )
    mark(two_away)
    two_got = swap(two_away, last_bit)
    one_mine, one_got = product_reduce(step(mixed_grad), weight_qkv, across)
    mark(one_mine)
    blocks = [one_block(k) for k in (1, 2)]
    over_x, over_y = add_corners(*step(*blocks, corner_a, corner_b))
    one_x, one_y = swap(over_x, 0), swap(over_y, 1)
    one_here = one_block(0)
    normed_one_grad = add_low(*step(one_mine, one_got))
    input_extra, gain_zero, bias_zero = norm_back(normed_one_grad, normal_zero, inv_zero, gain[0])
    inputs_grad = mark(middle_grad + input_extra)
    last_sums = step(last_sums)
    gain_three, bias_three = jnp.sum(last_sums[:8], axis=0), jnp.sum(last_sums[8:16], axis=0)
    squared = jnp.sum(last_sums[16:])
    sums = jnp.stack(
        [
            gain_zero, gain_one, gain_two, gain_three,
            bias_zero, bias_one, bias_two, bias_three,
        ],
        axis=0,
    )
    total = jnp.broadcast_to(squared, (8, 128))
    if groups == 2:
        sums = mark(jnp.concatenate([step(sums), total], axis=1))
        total = swap_core(sums)
    else:
        sums = lax.psum(jnp.concatenate([sums, total], axis=1), "tensor")
        total = jnp.zeros_like(sums)

    def send_sums(sums, total, bit):
        middle_column = sums.shape[1] // 2
        sent = mark(jnp.concatenate([sums[:, middle_column:], total], axis=1))
        return sums[:, :middle_column], total, swap(sent, bit)

    def take_sums(sums, total, got):
        got = step(got)
        return sums + got[:, : sums.shape[1]], total + got[:, sums.shape[1] :]

    two_got, *two_kept = step(two_got, *two_kept)
    two_away, two_kept = cut_z(two_kept + [two_got])
    mark(two_away)
    for bit in first_bits[:0:-1]:
        two_away, two_kept = cut_z(two_kept + [step(swap(two_away, bit))])
        mark(two_away)
    two_got = swap(two_away, first_bits[0])
    down_got, *down_kept = step(down_got, *down_kept)
    down = add_low(*down_kept, down_got)
    down_low = mark(low(down))
    sums, total = step(sums, total)
    sums = sums + total
    pending = send_sums(sums[:, :width], sums[:, width:], 1)
    two_got, *two_kept = step(two_got, *two_kept)
    two = mark(as_rows(add_low(*two_kept, two_got)))
    one_here, one_x, one_y = step(one_here, one_x, one_y)
    sums, total = take_sums(*pending)
    pending = send_sums(sums, total, 0)
    terms = [as_halves(t) for t in step(one_here, one_x, one_y)]
    one_away, one_kept = cut_z(terms)
    mark(one_away)
    sums, total = take_sums(*pending)
    middle_column = sums.shape[1] // 2
    sums = jnp.concatenate([sums[:, :middle_column], sums[:, middle_column:]], axis=0)
    total = jnp.concatenate([total, total], axis=0)

    def with_sums(away):
        sent = jnp.concatenate([sums[:, sums.shape[1] // 2 :], total], axis=1)
        sent = jnp.concatenate([sent[:8], sent[8:]], axis=1)
        high = low(sent)
        sent = jnp.concatenate([high, low(sent - high.astype(jnp.float32))], axis=1)
        columns_there = away.shape[2]
        sent = jnp.pad(sent, ((0, 0), (0, -sent.shape[1] % columns_there)))
        sent = jnp.split(sent, sent.shape[1] // columns_there, axis=1)
        return mark(jnp.concatenate([as_rows(away), *sent], axis=0))

    def take_both(got, rows):
        middle_column = sums.shape[1] // 2
        span = middle_column + total.shape[1]
        extra = got[rows:].astype(jnp.float32)
        extra = jnp.concatenate(jnp.split(extra, extra.shape[0] // 8, axis=0), axis=1)
        extra = extra[:, : 2 * span] + extra[:, 2 * span : 4 * span]
        extra = jnp.concatenate([extra[:, :span], extra[:, span:]], axis=0)
        return (
            got[:rows][None],
            sums[:, :middle_column] + extra[:, :middle_column],
            total + extra[:, middle_column:],
        )

    away_a, away_b = one_away[:1], one_away[1:]
    one_kept = mark(low(add_low(*one_kept)))
    kept_a, kept_b = [one_kept[:1]], [one_kept[1:]]
    got_a = swap(with_sums(away_a), last_bit)
    got_b = swap(mark(step(away_b)), last_bit)
    down_low = step(down_low)
    down_got = swap(down_low[1], 0), swap(down_low[3], 1)
    inputs_grad = step(inputs_grad)
    tokens_grad = mark(absolute(inputs_grad, lax.Precision.HIGHEST))
    for bit in first_bits[::-1]:
        got_a, *kept_a = step(got_a, *kept_a)
        got_a, sums, total = take_both(got_a, away_a.shape[1])
        away_a, kept_a = cut_z(kept_a + [got_a])
        got_a = swap(with_sums(away_a), bit)
        got_b, *kept_b = step(got_b, *kept_b)
        away_b, kept_b = cut_z(kept_b + [got_b])
        got_b = swap(mark(away_b), bit)
    layer_output = mark(low(absolute(step(result))))
    down_a, down_b = step(*down_got)
    down_part = mark(jnp.concatenate([add_low(down[0], down_a), add_low(down[2], down_b)], axis=0))
    got_a, *kept_a = step(got_a, *kept_a)
    got_a, sums, total = take_both(got_a, away_a.shape[1])
    got_b, *kept_b = step(got_b, *kept_b)
    small = lax.optimization_barrier(jnp.concatenate([sums[:8], sums[8:], total[:8]], axis=1))
    loss = small[0, small.shape[1] - 1] / (all_slots * width)
    own = width // (members * groups)
    sums = lax.dynamic_slice_in_dim(small, me * own, own, 1)

    def one_part(first):
        lanes = slice(first, first + local_width)
        return as_rows(
            jnp.concatenate(
                [
                    add_low(*[t[..., lanes] for t in kept_a], got_a[..., lanes]),
                    add_low(*[t[..., lanes] for t in kept_b], got_b[..., lanes]),
                ],
                axis=0,
            )
        )

    qkv_part = jnp.stack([one_part(out_width + k * local_width) for k in range(3)], axis=1)
    return (
        loss,
        layer_output,
        tokens_grad,
        qkv_part,
        one_part(0),
        two,
        down_part,
        sums[:4],
        sums[4:],
    )


def solution(mesh):
    return jax.shard_map(
        on_device,
        mesh=mesh,
        in_specs=(
            P(("dp", "tensor"), None),
            P(("dp", "tensor"), None),
            P("dp"),
            P("dp", None, "tensor"),
            P("dp", "tensor"),
            P("dp", "tensor"),
            P("dp", "tensor"),
            P(),
            P(),
        ),
        out_specs=(
            P(),
            P(("dp", "tensor"), None),
            P(("dp", "tensor"), None),
            P("dp", None, "tensor"),
            P("dp", "tensor"),
            P("dp", "tensor"),
            P("dp", "tensor"),
            P(None, ("dp", "tensor")),
            P(None, ("dp", "tensor")),
        ),
        check_vma=False,
    )
```

```python
import jax
import jax.numpy as jnp
from jax import lax
from jax.experimental import pallas as pl
from jax.experimental.pallas import tpu as pltpu
from jax.sharding import PartitionSpec as P

HEAD_DIM = 64


norm_eps = 1e-05


def norm_stats(values):
    center = values - jnp.mean(values, axis=-1, keepdims=True)
    spread = jnp.mean(center * center, axis=-1, keepdims=True)
    inv = lax.rsqrt(spread + norm_eps)
    return center * inv, inv


def norm_back(grad, normal, inv, gain):
    e = grad * gain
    back = inv * (
        e
        - jnp.mean(e, axis=-1, keepdims=True)
        - normal * jnp.mean(e * normal, axis=-1, keepdims=True)
    )
    return back, jnp.sum(grad * normal, axis=0), jnp.sum(grad, axis=0)


def rotate_pairs(values, cosine, sine):
    half_size = values.shape[-1] // 2
    front = values[..., :half_size]
    back_half = values[..., half_size:]
    return jnp.concatenate(
        [front * cosine - back_half * sine, back_half * cosine + front * sine], axis=-1
    )


def attend_forward(packed):
    queries, key_rows, value_rows, length, places = packed
    slot_count = queries.shape[0]
    block = min(512, slot_count)
    scale = HEAD_DIM ** (-0.5)
    outputs = []
    totals = []
    for begin in range(0, slot_count, block):
        finish = begin + block
        scores = (
            jnp.einsum(
                "qhd,khd->hqk",
                queries[begin:finish],
                key_rows,
                preferred_element_type=jnp.float32,
            )
            * scale
        )
        allowed = (places[None, :] <= places[begin:finish, None]) & (places[None, :] < length)
        scores = jnp.where(allowed[None], scores, -1000000000.0)
        top_score = jnp.max(scores, axis=-1, keepdims=True)
        weights = jnp.exp(scores - top_score)
        weight_sum = jnp.sum(weights, axis=-1, keepdims=True)
        probs = (weights / weight_sum).astype(jnp.bfloat16)
        outputs.append(
            jnp.einsum("hqk,khd->qhd", probs, value_rows, preferred_element_type=jnp.float32)
        )
        totals.append((top_score + jnp.log(weight_sum))[:, :, 0])
    return (jnp.concatenate(outputs, axis=0), jnp.concatenate(totals, axis=1))


def attend_probs(packed):
    queries, key_rows, totals, length, places = packed
    slot_count = queries.shape[0]
    block = min(512, slot_count)
    probs = []
    for begin in range(0, slot_count, block):
        finish = begin + block
        scores = jnp.einsum(
            "qhd,khd->hqk", queries[begin:finish], key_rows, preferred_element_type=jnp.float32
        ) * HEAD_DIM ** (-0.5)
        allowed = (places[None, :] <= places[begin:finish, None]) & (places[None, :] < length)
        weights = jnp.exp(scores - totals[:, begin:finish, None])
        probs.append(low(jnp.where(allowed[None], weights, 0.0)))
    return probs


def attend_backward(packed, probs_low, step, mark):
    queries, key_rows, value_rows, outputs, out_grads = packed
    slot_count = queries.shape[0]
    block = min(512, slot_count)
    scale = HEAD_DIM ** (-0.5)
    delta = jnp.sum(out_grads.astype(jnp.float32) * outputs, axis=-1).T
    key_grads = 0.0
    value_grads = 0.0
    query_grads = []

    def product(form, left, right):
        left, right = step(left, right)
        return mark(jnp.einsum(form, left, right, preferred_element_type=jnp.float32))

    for begin in range(0, slot_count, block):
        finish = begin + block
        query_block = queries[begin:finish]
        grad_block = step(out_grads[begin:finish])
        probs = probs_low[begin // block]
        prob_grads = jnp.einsum(
            "qhd,khd->hqk", grad_block, value_rows, preferred_element_type=jnp.float32
        )
        score_grads = mark(
            low(probs.astype(jnp.float32) * (prob_grads - delta[:, begin:finish, None]))
        )
        value_grads = value_grads + product("hqk,qhd->khd", probs, grad_block)
        query_grads.append(product("hqk,khd->qhd", score_grads, key_rows) * scale)
        key_grads = key_grads + product("hqk,qhd->khd", score_grads, query_block) * scale
    return (jnp.concatenate(query_grads, axis=0), key_grads, value_grads)


def swap(values, bit):
    size = lax.axis_size("dp")
    return lax.ppermute(values, "dp", [(j, j ^ (1 << bit)) for j in range(size)])


def swap_core(values):
    return lax.ppermute(values, "tensor", [(0, 1), (1, 0)])


def add_low(*terms):
    total = terms[0].astype(jnp.float32)
    for term in terms[1:]:
        total = total + term.astype(jnp.float32)
    return total


def low(values):
    return values.astype(jnp.bfloat16)


def after(values, *others):
    return lax.optimization_barrier((values,) + others)[0]


def matmul_t(rows, weight, first, tile=256):
    count, depth = rows.shape
    outs = weight.shape[0]

    def kernel(rows_ref, weight_ref, out_ref):
        out_ref[...] = low(
            lax.dot_general(
                rows_ref[...],
                weight_ref[:, first : first + depth],
                (((1,), (1,)), ((), ())),
                preferred_element_type=jnp.float32,
            )
        )

    return pl.pallas_call(
        kernel,
        grid=(outs // tile,),
        in_specs=[
            pl.BlockSpec((count, depth), lambda j: (0, 0)),
            pl.BlockSpec((tile, weight.shape[1]), lambda j: (j, 0)),
        ],
        out_specs=pl.BlockSpec((count, tile), lambda j: (0, j)),
        out_shape=jax.ShapeDtypeStruct((count, outs), jnp.bfloat16),
        compiler_params=pltpu.CompilerParams(vmem_limit_bytes=16 * 1024 * 1024),
        cost_estimate=pl.CostEstimate(
            flops=2 * count * depth * outs, bytes_accessed=2 * outs * depth, transcendentals=0
        ),
    )(rows, weight)


def last_norm(mine, got, middle, target, valid, gain, bias):
    count, width = middle.shape
    chunk = 16
    share = 1.0 / width

    def kernel(mine_ref, got_ref, middle_ref, target_ref, valid_ref, gain_ref, bias_ref, *outs):
        result_ref, grad_ref, back_ref, sums_ref = outs
        sums_ref[...] = jnp.zeros_like(sums_ref)
        gains = gain_ref[...]

        def body(i, carry):
            rows = pl.ds(pl.multiple_of(i * chunk, chunk), chunk)
            values = add_low(mine_ref[rows, :], got_ref[rows, :])
            center = values - jnp.sum(values, axis=-1, keepdims=True) * share
            spread = jnp.sum(center * center, axis=-1, keepdims=True) * share
            inv = lax.rsqrt(spread + norm_eps)
            normal = center * inv
            result = middle_ref[rows, :] + normal * gains + bias_ref[...]
            result_ref[rows, :] = low(result)
            error = result - target_ref[rows, :].astype(jnp.float32)
            grad = valid_ref[rows, :] * error
            grad_ref[rows, :] = grad
            e = grad * gains
            turned = grad * normal
            mean_one = jnp.sum(e, axis=-1, keepdims=True) * share
            mean_two = jnp.sum(turned * gains, axis=-1, keepdims=True) * share
            back_ref[rows, :] = low(inv * (e - mean_one - normal * mean_two))
            for k, term in enumerate((turned, grad, grad * error)):
                sums_ref[8 * k : 8 * k + 8, :] += term[:8] + term[8:]
            return carry

        lax.fori_loop(0, count // chunk, body, 0, unroll=4)

    return pl.pallas_call(
        kernel,
        in_specs=[pl.BlockSpec(memory_space=pltpu.VMEM)] * 7,
        out_specs=[pl.BlockSpec(memory_space=pltpu.VMEM)] * 4,
        out_shape=[
            jax.ShapeDtypeStruct((count, width), jnp.bfloat16),
            jax.ShapeDtypeStruct((count, width), jnp.float32),
            jax.ShapeDtypeStruct((count, width), jnp.bfloat16),
            jax.ShapeDtypeStruct((24, width), jnp.float32),
        ],
        compiler_params=pltpu.CompilerParams(vmem_limit_bytes=8 * 1024 * 1024),
        cost_estimate=pl.CostEstimate(
            flops=40 * count * width, bytes_accessed=18 * count * width, transcendentals=0
        ),
    )(mine, got, middle, target, valid, gain, bias)


class Chain:
    def __init__(self):
        self.last = ()

    def step(self, *values):
        if self.last:
            values = lax.optimization_barrier(tuple(values) + self.last)[: len(values)]
        return values[0] if len(values) == 1 else tuple(values)

    def mark(self, *values):
        self.last = values
        return values[0] if len(values) == 1 else values


def relative_map(members, width):
    bits = members.bit_length() - 1
    block = width // members
    half = block // 2
    rel = jnp.arange(width)
    place = rel // half
    mask = jnp.zeros_like(rel)
    for k, bit in enumerate(range(bits - 1, 1, -1)):
        mask = mask | (((place >> k) & 1) << bit)
    side = (place >> (bits - 2)) & 1
    mask = mask | ((place >> (bits - 1)) & 3)
    source = (lax.axis_index("dp") ^ mask) * block + side * half + rel % half
    return (jnp.arange(width)[:, None] == source[None, :]).astype(jnp.bfloat16)


def high_bits():
    return tuple(range(lax.axis_size("dp").bit_length() - 2, 1, -1))


def as_halves(part):
    return part.reshape(2, part.shape[0] // 2, part.shape[1])


def as_rows(part):
    return part.reshape(-1, part.shape[-1])


def join_rows(*pieces):
    return lax.optimization_barrier(jnp.concatenate(pieces, axis=0))


def columns(left, *which):
    step = left.shape[1] // 8
    parts = [left[:, k * step : (k + 1) * step] for k in which]
    return parts[0] if len(parts) == 1 else jnp.concatenate(parts, axis=1)


def quarter(left, k):
    step = left.shape[1] // 4
    return left[:, k * step : (k + 1) * step]


def product_t(left, right):
    return low(
        lax.dot_general(left, right, (((0,), (0,)), ((), ())), preferred_element_type=jnp.float32)
    )


def collect_rows(values):
    if lax.axis_size("tensor") != 2:
        return lax.all_gather(values, "tensor", axis=0, tiled=True)
    return jnp.concatenate([values, swap_core(values)], axis=0)


def product_reduce(inputs, weight, dims, first=None):
    def product(rows):
        if first is not None:
            return matmul_t(rows, weight, first)
        return low(lax.dot_general(rows, weight, dims, preferred_element_type=jnp.float32))

    if lax.axis_size("tensor") != 2:
        return (
            lax.psum_scatter(product(inputs), "tensor", scatter_dimension=0, tiled=True),
            jnp.zeros((), jnp.bfloat16),
        )
    own_rows = inputs.shape[0] // 2
    got = swap_core(product(inputs[own_rows:]))
    return product(inputs[:own_rows]), got


def on_device(tokens, teacher, lengths, w_qkv, w_out, w_up, w_down, norm_gain, norm_bias):
    chain = Chain()
    step, mark = chain.step, chain.mark
    tok_dev, width = tokens.shape
    groups = lax.axis_size("tensor")
    members = lax.axis_size("dp")
    row_count = lengths.shape[0]
    group_tokens = tok_dev * groups
    slot_count = group_tokens // row_count
    all_slots = group_tokens * members
    me = lax.axis_index("tensor")
    own_places = me * tok_dev + jnp.arange(tok_dev)
    if groups == 2 and row_count == 1:
        places = jnp.concatenate([own_places, (1 - me) * tok_dev + jnp.arange(tok_dev)])
    else:
        places = jnp.arange(group_tokens)
    row_index = own_places // slot_count
    row_length = jnp.sum(
        jnp.where(row_index[:, None] == jnp.arange(row_count)[None, :], lengths[None, :], 0), axis=1
    )
    valid = (own_places % slot_count < row_length).astype(jnp.float32)[:, None]
    row_places = (places % slot_count).reshape(row_count, slot_count)
    angles = row_places[0].astype(jnp.float32)[:, None] * (
        10000.0 ** (-2.0 * jnp.arange(HEAD_DIM // 2).astype(jnp.float32) / HEAD_DIM)
    )
    cosine, sine = jnp.cos(angles)[:, None, :], jnp.sin(angles)[:, None, :]
    local_width = w_qkv.shape[2]
    heads_here = local_width // HEAD_DIM
    out_width = w_out.shape[1]
    hidden_width = w_up.shape[1]
    bits = high_bits()
    across = (((1,), (1,)), ((), ()))

    first_bits, last_bit = bits[:-1], bits[-1]

    def gather_first_z(part):
        for bit in first_bits:
            got = swap(part, bit)
            part = mark(jnp.concatenate(step(part, got), axis=1))
        return part

    def gather_last_z(part, got):
        return mark(jnp.concatenate(step(part, got), axis=1))

    def cut_z(terms):
        cut = terms[0].shape[1] // 2
        away = low(add_low(*[t[:, cut:] for t in terms]))
        return away, [t[:, :cut] for t in terms]

    def add_all_z(away, kept):
        terms = kept + [swap(away, last_bit)]
        for bit in first_bits[::-1]:
            away, kept = cut_z(list(step(*terms)))
            mark(away)
            terms = kept + [swap(away, bit)]
        return terms

    to_rel = relative_map(members, width)

    def relative(values):
        return jnp.dot(values, to_rel, preferred_element_type=jnp.float32)

    def absolute(values, precision=None):
        return lax.dot_general(
            values,
            to_rel.astype(values.dtype),
            (((1,), (1,)), ((), ())),
            precision=precision,
            preferred_element_type=jnp.float32,
        )

    def both(mine, got):
        return jnp.concatenate([mine, got], axis=0)

    def swap_rows(values):
        if groups == 2:
            return values, swap_core(values)
        every = lax.all_gather(values, "tensor", axis=0, tiled=True)
        return every, every[:0]

    one = as_halves(w_qkv.reshape(w_qkv.shape[0], 3 * local_width))
    two = as_halves(jnp.concatenate([w_out, w_up], axis=1))
    three_a, three_b = as_halves(w_down)
    three_got = swap(three_a, 0), swap(three_b, 1)
    one_a, one_b = one[:1], one[1:]
    counted = [jnp.sum(lengths).astype(jnp.float32).reshape(1, 1)]
    to_count = [0, bits[0], 1, *bits[1:]]

    def count_more():
        total = counted[-1]
        if len(counted) > 1:
            total = mark(sum(step(*counted)))
        counted[:] = [total, swap(total, to_count.pop(0))] if to_count else [total]

    count_more()
    got_a, got_b = swap(one_a, first_bits[0]), swap(one_b, first_bits[0])
    one_a = mark(jnp.concatenate(step(one_a, got_a), axis=1))
    for bit in first_bits[1:]:
        one_a = mark(jnp.concatenate(step(one_a, swap(one_a, bit)), axis=1))
    got_a = swap(one_a, last_bit)
    count_more()
    one_b = mark(jnp.concatenate(step(one_b, got_b), axis=1))
    for bit in first_bits[1:]:
        one_b = mark(jnp.concatenate(step(one_b, swap(one_b, bit)), axis=1))
    got_b = swap(one_b, last_bit)
    count_more()
    tokens, teacher, norm_gain, norm_bias = step(tokens, teacher, norm_gain, norm_bias)
    inputs = relative(tokens)
    target = low(relative(teacher))
    affine = jnp.dot(
        jnp.concatenate([norm_gain, norm_bias], axis=0),
        to_rel.astype(jnp.float32),
        precision=lax.Precision.HIGHEST,
        preferred_element_type=jnp.float32,
    )
    gain, bias = affine[:4], affine[4:]
    normal_zero, inv_zero = norm_stats(inputs)
    rows_one, other_one = swap_rows(mark(low(normal_zero * gain[0] + bias[0])))
    one = step(one_a, got_a, one_b, got_b)
    one = mark(jnp.concatenate([as_rows(p) for p in one], axis=0))
    one_x, one_y = swap(one, 0), swap(one, 1)
    count_more()
    two = step(two)
    for bit in first_bits[:1]:
        two_got = swap(two, bit)
    three_a, three_b, three_xa, three_yb = step(three_a, three_b, *three_got)
    three_a, three_b = mark(jnp.stack([three_a, three_xa]), jnp.stack([three_b, three_yb]))
    two = mark(jnp.concatenate(step(two, two_got), axis=1))
    for bit in first_bits[1:]:
        two = mark(jnp.concatenate(step(two, swap(two, bit)), axis=1))
    two_got = swap(two, last_bit)
    three_a, three_b = step(three_a, three_b)
    three_got = swap(three_a, first_bits[0]), swap(three_b, first_bits[0])

    def high_steps(part, got):
        part = mark(jnp.concatenate(step(part, got), axis=1))
        for bit in first_bits[1:]:
            part = mark(jnp.concatenate(step(part, swap(part, bit)), axis=1))
        return part, swap(part, last_bit)

    cut = one.shape[0] // 2
    one_x, one_y = step(one_x, one_y)
    corner_a, corner_b = mark(one_x[:cut], one_y[cut:])
    corner_a, corner_b = swap(corner_a, 1), swap(corner_b, 0)
    two = mark(as_rows(jnp.concatenate(step(two, two_got), axis=1)))
    two_x, two_y = swap(two, 0), swap(two, 1)
    one, other_one, corner_a, corner_b = step(one, other_one, corner_a, corner_b)
    weight_qkv = join_rows(one, one_x, one_y, corner_a, corner_b)
    rows_one = both(rows_one, other_one)
    mixed = jnp.dot(rows_one, weight_qkv, preferred_element_type=jnp.float32)
    mixed = mixed.reshape(row_count, slot_count, 3, heads_here, HEAD_DIM)
    queries = low(rotate_pairs(mixed[:, :, 0], cosine, sine))
    key_rows = low(rotate_pairs(mixed[:, :, 1], cosine, sine))
    value_rows = low(mixed[:, :, 2])
    attended, totals = lax.map(
        attend_forward, (queries, key_rows, value_rows, lengths, row_places)
    )
    attended_low = mark(low(attended.reshape(group_tokens, local_width)))
    while len(counted) > 1:
        count_more()
    weight = valid * (all_slots / counted[0])
    three_a, got_a = high_steps(three_a, three_got[0])
    three_b, got_b = high_steps(three_b, three_got[1])
    two_x, two_y = step(two_x, two_y)
    corner_a, corner_b = mark(two_x[:cut], two_y[cut:])
    corner_a, corner_b = swap(corner_a, 1), swap(corner_b, 0)
    three_a, three_b = gather_last_z(three_a, got_a), gather_last_z(three_b, got_b)
    last_a, last_b = swap(three_a, 1), swap(three_b, 0)
    two, corner_a, corner_b = step(two, corner_a, corner_b)
    weight_mid = mark(join_rows(two, two_x, two_y, corner_a, corner_b))
    weight_out, weight_up = weight_mid[:, :out_width], weight_mid[:, out_width:]
    attn_mine, attn_got = product_reduce(attended_low, weight_out, across)
    mark(attn_mine)
    attn_sum = add_low(*step(attn_mine, attn_got))
    normal_one, inv_one = norm_stats(attn_sum)
    middle = inputs + normal_one * gain[1] + bias[1]
    normal_two, inv_two = norm_stats(middle)
    rows_two, other_two = swap_rows(mark(low(normal_two * gain[2] + bias[2])))
    rows_two = both(*step(rows_two, other_two))
    hidden = jnp.dot(rows_two, weight_up, preferred_element_type=jnp.float32)
    half = 0.5 * (1.0 + lax.erf(hidden * (2.0**-0.5)))
    active = low(hidden * half)
    slope = low(half + hidden * jnp.exp(-0.5 * hidden * hidden) * ((2.0 * jnp.pi) ** -0.5))
    active, slope = mark(*lax.optimization_barrier((active, slope)))
    (y_a0, y_a1), (x_b0, x_b1) = step(last_a, last_b)
    weight_down = mark(
        join_rows(three_a[0], three_b[0], three_a[1], x_b0, y_a0, three_b[1], y_a1, x_b1)
    )
    mine, got = product_reduce(active, weight_down, across)
    mark(mine)
    mine, got = step(mine, jnp.broadcast_to(got, mine.shape))
    result, out_grad, mlp_grad, last_sums = last_norm(
        mine, got, middle, target, weight, gain[3:4], bias[3:4]
    )
    mlp_rows, other = swap_rows(mark(mlp_grad))
    mlp_rows = both(*step(mlp_rows, other))

    def down_block(k):
        return mark(product_t(columns(step(mlp_rows), k), active))

    away = down_block(4), down_block(3)
    early = swap(away[0], 1), swap(away[1], 0)
    away = down_block(6), down_block(7)
    late = swap(away[0], 1), swap(away[1], 0)
    active_grad = jnp.dot(step(mlp_rows), weight_down, preferred_element_type=jnp.float32)
    hidden_grad = mark(low(active_grad * slope.astype(jnp.float32)))
    two_mine, two_got = product_reduce(hidden_grad, weight_mid, across, out_width)
    mark(two_mine)
    block = mark(product_t(quarter(step(rows_two), 3), hidden_grad))
    early = step(*early)
    corner_a, corner_b = swap(block[:cut], 1), swap(block[cut:], 0)
    kept = [down_block(k) for k in (0, 2, 1, 5)]
    normed_two_grad = add_low(*step(two_mine, two_got))
    middle_extra, gain_two, bias_two = norm_back(normed_two_grad, normal_two, inv_two, gain[2])
    middle_grad = out_grad + middle_extra
    attn_grad, gain_one, bias_one = norm_back(middle_grad, normal_one, inv_one, gain[1])
    attn_rows, other = swap_rows(mark(low(attn_grad)))
    def up_block(k):
        return mark(product_t(columns(step(rows_two), k), hidden_grad))

    side_b, side_a = up_block(3), up_block(4)
    two_xb, two_ya = swap(side_b, 0), swap(side_a, 1)
    side_a, side_b = up_block(2), up_block(5)
    two_here = mark(product_t(quarter(step(rows_two), 0), hidden_grad))
    late = step(*late)
    down = jnp.stack(
        [low(add_low(k, g)) for k, g in zip(kept, (early[0], late[0], early[1], late[1]))], axis=0
    )
    down_away, down_kept = cut_z([down])
    mark(down_away)
    down_got = swap(down_away, last_bit)
    queries_now, totals_now = step(queries, totals)
    probs_low = [
        attend_probs(
            tuple(v[row] for v in (queries_now, key_rows, totals_now, lengths, row_places))
        )
        for row in range(row_count)
    ]
    mark(*[p for row in probs_low for p in row])
    attn_rows = both(*step(attn_rows, other))
    attended_grad = mark(
        low(jnp.dot(attn_rows, weight_out, preferred_element_type=jnp.float32))
    ).reshape(row_count, slot_count, heads_here, HEAD_DIM)

    side_a = mark(low(add_low(side_a, step(corner_a))))
    side_b = mark(low(add_low(side_b, step(corner_b))))
    two_xa, two_yb = swap(side_a, 0), swap(side_b, 1)
    grads = [
        attend_backward(
            tuple(v[row] for v in (queries, key_rows, value_rows, attended, attended_grad)),
            probs_low[row],
            step,
            mark,
        )
        for row in range(row_count)
    ]
    query_grads, key_grads, value_grads = (jnp.stack(g, axis=0) for g in zip(*grads))
    query_grads, key_grads, value_grads = step(query_grads, key_grads, value_grads)
    mixed_grad = jnp.stack(
        [
            rotate_pairs(query_grads, cosine, -sine),
            rotate_pairs(key_grads, cosine, -sine),
            value_grads,
        ],
        axis=2,
    )
    mixed_grad = mark(low(mixed_grad.reshape(group_tokens, 3 * local_width)))

    def add_corners(over_x, over_y, from_y, from_x):
        over_x = jnp.concatenate([low(add_low(over_x[:cut], from_y)), over_x[cut:]], axis=0)
        over_y = jnp.concatenate([over_y[:cut], low(add_low(over_y[cut:], from_x))], axis=0)
        return mark(over_x, over_y)

    def one_block(k):
        left, right = step(attn_rows, rows_one)
        return mark(
            jnp.concatenate(
                [
                    product_t(quarter(left, k), attended_low),
                    product_t(quarter(right, k), mixed_grad),
                ],
                axis=1,
            )
        )

    block = one_block(3)
    down_got, *down_kept = step(down_got, *down_kept)
    down_away, down_kept = cut_z(down_kept + [down_got])
    mark(down_away)
    for bit in first_bits[:0:-1]:
        down_away, down_kept = cut_z(down_kept + [step(swap(down_away, bit))])
        mark(down_away)
    down_got = swap(down_away, first_bits[0])
    two_xa, two_xb, two_ya, two_yb = step(two_xa, two_xb, two_ya, two_yb)
    corner_a, corner_b = swap(block[:cut], 1), swap(block[cut:], 0)
    two_away, two_kept = cut_z(
        [as_halves(two_here), jnp.stack([two_xa, two_xb]), jnp.stack([two_ya, two_yb])]
    )
    mark(two_away)
    two_got = swap(two_away, last_bit)
    one_mine, one_got = product_reduce(step(mixed_grad), weight_qkv, across)
    mark(one_mine)
    blocks = [one_block(k) for k in (1, 2)]
    over_x, over_y = add_corners(*step(*blocks, corner_a, corner_b))
    one_x, one_y = swap(over_x, 0), swap(over_y, 1)
    one_here = one_block(0)
    normed_one_grad = add_low(*step(one_mine, one_got))
    input_extra, gain_zero, bias_zero = norm_back(normed_one_grad, normal_zero, inv_zero, gain[0])
    inputs_grad = mark(middle_grad + input_extra)
    last_sums = step(last_sums)
    gain_three, bias_three = jnp.sum(last_sums[:8], axis=0), jnp.sum(last_sums[8:16], axis=0)
    squared = jnp.sum(last_sums[16:])
    sums = jnp.stack(
        [
            gain_zero, gain_one, gain_two, gain_three,
            bias_zero, bias_one, bias_two, bias_three,
        ],
        axis=0,
    )
    total = jnp.broadcast_to(squared, (8, 128))
    if groups == 2:
        sums = mark(jnp.concatenate([step(sums), total], axis=1))
        total = swap_core(sums)
    else:
        sums = lax.psum(jnp.concatenate([sums, total], axis=1), "tensor")
        total = jnp.zeros_like(sums)

    def send_sums(sums, total, bit):
        middle_column = sums.shape[1] // 2
        sent = mark(jnp.concatenate([sums[:, middle_column:], total], axis=1))
        return sums[:, :middle_column], total, swap(sent, bit)

    def take_sums(sums, total, got):
        got = step(got)
        return sums + got[:, : sums.shape[1]], total + got[:, sums.shape[1] :]

    two_got, *two_kept = step(two_got, *two_kept)
    two_away, two_kept = cut_z(two_kept + [two_got])
    mark(two_away)
    for bit in first_bits[:0:-1]:
        two_away, two_kept = cut_z(two_kept + [step(swap(two_away, bit))])
        mark(two_away)
    two_got = swap(two_away, first_bits[0])
    down_got, *down_kept = step(down_got, *down_kept)
    down = add_low(*down_kept, down_got)
    down_low = mark(low(down))
    sums, total = step(sums, total)
    sums = sums + total
    pending = send_sums(sums[:, :width], sums[:, width:], 1)
    two_got, *two_kept = step(two_got, *two_kept)
    two = mark(as_rows(add_low(*two_kept, two_got)))
    one_here, one_x, one_y = step(one_here, one_x, one_y)
    sums, total = take_sums(*pending)
    pending = send_sums(sums, total, 0)
    terms = [as_halves(t) for t in step(one_here, one_x, one_y)]
    one_away, one_kept = cut_z(terms)
    mark(one_away)
    sums, total = take_sums(*pending)
    middle_column = sums.shape[1] // 2
    sums = jnp.concatenate([sums[:, :middle_column], sums[:, middle_column:]], axis=0)
    total = jnp.concatenate([total, total], axis=0)

    def with_sums(away):
        sent = jnp.concatenate([sums[:, sums.shape[1] // 2 :], total], axis=1)
        sent = jnp.concatenate([sent[:8], sent[8:]], axis=1)
        high = low(sent)
        sent = jnp.concatenate([high, low(sent - high.astype(jnp.float32))], axis=1)
        columns_there = away.shape[2]
        sent = jnp.pad(sent, ((0, 0), (0, -sent.shape[1] % columns_there)))
        sent = jnp.split(sent, sent.shape[1] // columns_there, axis=1)
        return mark(jnp.concatenate([as_rows(away), *sent], axis=0))

    def take_both(got, rows):
        middle_column = sums.shape[1] // 2
        span = middle_column + total.shape[1]
        extra = got[rows:].astype(jnp.float32)
        extra = jnp.concatenate(jnp.split(extra, extra.shape[0] // 8, axis=0), axis=1)
        extra = extra[:, : 2 * span] + extra[:, 2 * span : 4 * span]
        extra = jnp.concatenate([extra[:, :span], extra[:, span:]], axis=0)
        return (
            got[:rows][None],
            sums[:, :middle_column] + extra[:, :middle_column],
            total + extra[:, middle_column:],
        )

    away_a, away_b = one_away[:1], one_away[1:]
    one_kept = mark(low(add_low(*one_kept)))
    kept_a, kept_b = [one_kept[:1]], [one_kept[1:]]
    got_a = swap(with_sums(away_a), last_bit)
    got_b = swap(mark(step(away_b)), last_bit)
    down_low = step(down_low)
    down_got = swap(down_low[1], 0), swap(down_low[3], 1)
    inputs_grad = step(inputs_grad)
    tokens_grad = mark(absolute(inputs_grad, lax.Precision.HIGHEST))
    for bit in first_bits[::-1]:
        got_a, *kept_a = step(got_a, *kept_a)
        got_a, sums, total = take_both(got_a, away_a.shape[1])
        away_a, kept_a = cut_z(kept_a + [got_a])
        got_a = swap(with_sums(away_a), bit)
        got_b, *kept_b = step(got_b, *kept_b)
        away_b, kept_b = cut_z(kept_b + [got_b])
        got_b = swap(mark(away_b), bit)
    layer_output = mark(low(absolute(step(result))))
    down_a, down_b = step(*down_got)
    down_part = mark(jnp.concatenate([add_low(down[0], down_a), add_low(down[2], down_b)], axis=0))
    got_a, *kept_a = step(got_a, *kept_a)
    got_a, sums, total = take_both(got_a, away_a.shape[1])
    got_b, *kept_b = step(got_b, *kept_b)
    small = lax.optimization_barrier(jnp.concatenate([sums[:8], sums[8:], total[:8]], axis=1))
    loss = small[0, small.shape[1] - 1] / (all_slots * width)
    own = width // (members * groups)
    sums = lax.dynamic_slice_in_dim(small, me * own, own, 1)

    def one_part(first):
        lanes = slice(first, first + local_width)
        return as_rows(
            jnp.concatenate(
                [
                    add_low(*[t[..., lanes] for t in kept_a], got_a[..., lanes]),
                    add_low(*[t[..., lanes] for t in kept_b], got_b[..., lanes]),
                ],
                axis=0,
            )
        )

    qkv_part = jnp.stack([one_part(out_width + k * local_width) for k in range(3)], axis=1)
    return (
        loss,
        layer_output,
        tokens_grad,
        qkv_part,
        one_part(0),
        two,
        down_part,
        sums[:4],
        sums[4:],
    )


def solution(mesh):
    return jax.shard_map(
        on_device,
        mesh=mesh,
        in_specs=(
            P(("dp", "tensor"), None),
            P(("dp", "tensor"), None),
            P("dp"),
            P("dp", None, "tensor"),
            P("dp", "tensor"),
            P("dp", "tensor"),
            P("dp", "tensor"),
            P(),
            P(),
        ),
        out_specs=(
            P(),
            P(("dp", "tensor"), None),
            P(("dp", "tensor"), None),
            P("dp", None, "tensor"),
            P("dp", "tensor"),
            P("dp", "tensor"),
            P("dp", "tensor"),
            P(None, ("dp", "tensor")),
            P(None, ("dp", "tensor")),
        ),
        check_vma=False,
    )
```

```python
import jax
import jax.numpy as jnp
from jax import lax
from jax.experimental import pallas as pl
from jax.experimental.pallas import tpu as pltpu
from jax.sharding import PartitionSpec as P

HEAD_DIM = 64


norm_eps = 1e-05


def norm_stats(values):
    center = values - jnp.mean(values, axis=-1, keepdims=True)
    spread = jnp.mean(center * center, axis=-1, keepdims=True)
    inv = lax.rsqrt(spread + norm_eps)
    return center * inv, inv


def norm_back(grad, normal, inv, gain):
    e = grad * gain
    back = inv * (
        e
        - jnp.mean(e, axis=-1, keepdims=True)
        - normal * jnp.mean(e * normal, axis=-1, keepdims=True)
    )
    return back, jnp.sum(grad * normal, axis=0), jnp.sum(grad, axis=0)


def rotate_pairs(values, cosine, sine):
    half_size = values.shape[-1] // 2
    front = values[..., :half_size]
    back_half = values[..., half_size:]
    return jnp.concatenate(
        [front * cosine - back_half * sine, back_half * cosine + front * sine], axis=-1
    )


def attend_forward(packed):
    queries, key_rows, value_rows, length, places = packed
    slot_count = queries.shape[0]
    block = min(512, slot_count)
    scale = HEAD_DIM ** (-0.5)
    outputs = []
    totals = []
    for begin in range(0, slot_count, block):
        finish = begin + block
        scores = (
            jnp.einsum(
                "qhd,khd->hqk",
                queries[begin:finish],
                key_rows,
                preferred_element_type=jnp.float32,
            )
            * scale
        )
        allowed = (places[None, :] <= places[begin:finish, None]) & (places[None, :] < length)
        scores = jnp.where(allowed[None], scores, -1000000000.0)
        top_score = jnp.max(scores, axis=-1, keepdims=True)
        weights = jnp.exp(scores - top_score)
        weight_sum = jnp.sum(weights, axis=-1, keepdims=True)
        probs = (weights / weight_sum).astype(jnp.bfloat16)
        outputs.append(
            jnp.einsum("hqk,khd->qhd", probs, value_rows, preferred_element_type=jnp.float32)
        )
        totals.append((top_score + jnp.log(weight_sum))[:, :, 0])
    return (jnp.concatenate(outputs, axis=0), jnp.concatenate(totals, axis=1))


def attend_probs(packed):
    queries, key_rows, totals, length, places = packed
    slot_count = queries.shape[0]
    block = min(512, slot_count)
    probs = []
    for begin in range(0, slot_count, block):
        finish = begin + block
        scores = jnp.einsum(
            "qhd,khd->hqk", queries[begin:finish], key_rows, preferred_element_type=jnp.float32
        ) * HEAD_DIM ** (-0.5)
        allowed = (places[None, :] <= places[begin:finish, None]) & (places[None, :] < length)
        weights = jnp.exp(scores - totals[:, begin:finish, None])
        probs.append(low(jnp.where(allowed[None], weights, 0.0)))
    return probs


def attend_backward(packed, probs_low, step, mark):
    queries, key_rows, value_rows, outputs, out_grads = packed
    slot_count = queries.shape[0]
    block = min(512, slot_count)
    scale = HEAD_DIM ** (-0.5)
    delta = jnp.sum(out_grads.astype(jnp.float32) * outputs, axis=-1).T
    key_grads = 0.0
    value_grads = 0.0
    query_grads = []

    def product(form, left, right):
        left, right = step(left, right)
        return mark(jnp.einsum(form, left, right, preferred_element_type=jnp.float32))

    for begin in range(0, slot_count, block):
        finish = begin + block
        query_block = queries[begin:finish]
        grad_block = step(out_grads[begin:finish])
        probs = probs_low[begin // block]
        prob_grads = jnp.einsum(
            "qhd,khd->hqk", grad_block, value_rows, preferred_element_type=jnp.float32
        )
        score_grads = mark(
            low(probs.astype(jnp.float32) * (prob_grads - delta[:, begin:finish, None]))
        )
        value_grads = value_grads + product("hqk,qhd->khd", probs, grad_block)
        query_grads.append(product("hqk,khd->qhd", score_grads, key_rows) * scale)
        key_grads = key_grads + product("hqk,qhd->khd", score_grads, query_block) * scale
    return (jnp.concatenate(query_grads, axis=0), key_grads, value_grads)


def swap(values, bit):
    size = lax.axis_size("dp")
    return lax.ppermute(values, "dp", [(j, j ^ (1 << bit)) for j in range(size)])


def swap_core(values):
    return lax.ppermute(values, "tensor", [(0, 1), (1, 0)])


def add_low(*terms):
    total = terms[0].astype(jnp.float32)
    for term in terms[1:]:
        total = total + term.astype(jnp.float32)
    return total


def low(values):
    return values.astype(jnp.bfloat16)


def after(values, *others):
    return lax.optimization_barrier((values,) + others)[0]


def matmul_t(rows, weight, first, tile=256):
    count, depth = rows.shape
    outs = weight.shape[0]

    def kernel(rows_ref, weight_ref, out_ref):
        out_ref[...] = low(
            lax.dot_general(
                rows_ref[...],
                weight_ref[:, first : first + depth],
                (((1,), (1,)), ((), ())),
                preferred_element_type=jnp.float32,
            )
        )

    return pl.pallas_call(
        kernel,
        grid=(outs // tile,),
        in_specs=[
            pl.BlockSpec((count, depth), lambda j: (0, 0)),
            pl.BlockSpec((tile, weight.shape[1]), lambda j: (j, 0)),
        ],
        out_specs=pl.BlockSpec((count, tile), lambda j: (0, j)),
        out_shape=jax.ShapeDtypeStruct((count, outs), jnp.bfloat16),
        compiler_params=pltpu.CompilerParams(vmem_limit_bytes=16 * 1024 * 1024),
        cost_estimate=pl.CostEstimate(
            flops=2 * count * depth * outs, bytes_accessed=2 * outs * depth, transcendentals=0
        ),
    )(rows, weight)


def last_norm(mine, got, middle, target, valid, gain, bias):
    count, width = middle.shape
    chunk = 16
    share = 1.0 / width

    def kernel(mine_ref, got_ref, middle_ref, target_ref, valid_ref, gain_ref, bias_ref, *outs):
        result_ref, grad_ref, back_ref, sums_ref = outs
        sums_ref[...] = jnp.zeros_like(sums_ref)
        gains = gain_ref[...]

        def body(i, carry):
            rows = pl.ds(pl.multiple_of(i * chunk, chunk), chunk)
            values = add_low(mine_ref[rows, :], got_ref[rows, :])
            center = values - jnp.sum(values, axis=-1, keepdims=True) * share
            spread = jnp.sum(center * center, axis=-1, keepdims=True) * share
            inv = lax.rsqrt(spread + norm_eps)
            normal = center * inv
            result = middle_ref[rows, :] + normal * gains + bias_ref[...]
            result_ref[rows, :] = low(result)
            error = result - target_ref[rows, :].astype(jnp.float32)
            grad = valid_ref[rows, :] * error
            grad_ref[rows, :] = grad
            e = grad * gains
            turned = grad * normal
            mean_one = jnp.sum(e, axis=-1, keepdims=True) * share
            mean_two = jnp.sum(turned * gains, axis=-1, keepdims=True) * share
            back_ref[rows, :] = low(inv * (e - mean_one - normal * mean_two))
            for k, term in enumerate((turned, grad, grad * error)):
                sums_ref[8 * k : 8 * k + 8, :] += term[:8] + term[8:]
            return carry

        lax.fori_loop(0, count // chunk, body, 0, unroll=4)

    return pl.pallas_call(
        kernel,
        in_specs=[pl.BlockSpec(memory_space=pltpu.VMEM)] * 7,
        out_specs=[pl.BlockSpec(memory_space=pltpu.VMEM)] * 4,
        out_shape=[
            jax.ShapeDtypeStruct((count, width), jnp.bfloat16),
            jax.ShapeDtypeStruct((count, width), jnp.float32),
            jax.ShapeDtypeStruct((count, width), jnp.bfloat16),
            jax.ShapeDtypeStruct((24, width), jnp.float32),
        ],
        compiler_params=pltpu.CompilerParams(vmem_limit_bytes=8 * 1024 * 1024),
        cost_estimate=pl.CostEstimate(
            flops=40 * count * width, bytes_accessed=18 * count * width, transcendentals=0
        ),
    )(mine, got, middle, target, valid, gain, bias)


class Chain:
    def __init__(self):
        self.last = ()

    def step(self, *values):
        if self.last:
            values = lax.optimization_barrier(tuple(values) + self.last)[: len(values)]
        return values[0] if len(values) == 1 else tuple(values)

    def mark(self, *values):
        self.last = values
        return values[0] if len(values) == 1 else values


def relative_map(members, width):
    bits = members.bit_length() - 1
    block = width // members
    half = block // 2
    rel = jnp.arange(width)
    place = rel // half
    mask = jnp.zeros_like(rel)
    for k, bit in enumerate(range(bits - 1, 1, -1)):
        mask = mask | (((place >> k) & 1) << bit)
    side = (place >> (bits - 2)) & 1
    mask = mask | ((place >> (bits - 1)) & 3)
    source = (lax.axis_index("dp") ^ mask) * block + side * half + rel % half
    return (jnp.arange(width)[:, None] == source[None, :]).astype(jnp.bfloat16)


def high_bits():
    return tuple(range(lax.axis_size("dp").bit_length() - 2, 1, -1))


def as_halves(part):
    return part.reshape(2, part.shape[0] // 2, part.shape[1])


def as_rows(part):
    return part.reshape(-1, part.shape[-1])


def join_rows(*pieces):
    return lax.optimization_barrier(jnp.concatenate(pieces, axis=0))


def columns(left, *which):
    step = left.shape[1] // 8
    parts = [left[:, k * step : (k + 1) * step] for k in which]
    return parts[0] if len(parts) == 1 else jnp.concatenate(parts, axis=1)


def quarter(left, k):
    step = left.shape[1] // 4
    return left[:, k * step : (k + 1) * step]


def product_t(left, right):
    return low(
        lax.dot_general(left, right, (((0,), (0,)), ((), ())), preferred_element_type=jnp.float32)
    )


def collect_rows(values):
    if lax.axis_size("tensor") != 2:
        return lax.all_gather(values, "tensor", axis=0, tiled=True)
    return jnp.concatenate([values, swap_core(values)], axis=0)


def product_reduce(inputs, weight, dims, first=None):
    def product(rows):
        if first is not None:
            return matmul_t(rows, weight, first)
        return low(lax.dot_general(rows, weight, dims, preferred_element_type=jnp.float32))

    if lax.axis_size("tensor") != 2:
        return (
            lax.psum_scatter(product(inputs), "tensor", scatter_dimension=0, tiled=True),
            jnp.zeros((), jnp.bfloat16),
        )
    own_rows = inputs.shape[0] // 2
    got = swap_core(product(inputs[own_rows:]))
    return product(inputs[:own_rows]), got


def on_device(tokens, teacher, lengths, w_qkv, w_out, w_up, w_down, norm_gain, norm_bias):
    chain = Chain()
    step, mark = chain.step, chain.mark
    tok_dev, width = tokens.shape
    groups = lax.axis_size("tensor")
    members = lax.axis_size("dp")
    row_count = lengths.shape[0]
    group_tokens = tok_dev * groups
    slot_count = group_tokens // row_count
    all_slots = group_tokens * members
    me = lax.axis_index("tensor")
    own_places = me * tok_dev + jnp.arange(tok_dev)
    if groups == 2 and row_count == 1:
        places = jnp.concatenate([own_places, (1 - me) * tok_dev + jnp.arange(tok_dev)])
    else:
        places = jnp.arange(group_tokens)
    row_index = own_places // slot_count
    row_length = jnp.sum(
        jnp.where(row_index[:, None] == jnp.arange(row_count)[None, :], lengths[None, :], 0), axis=1
    )
    valid = (own_places % slot_count < row_length).astype(jnp.float32)[:, None]
    row_places = (places % slot_count).reshape(row_count, slot_count)
    angles = row_places[0].astype(jnp.float32)[:, None] * (
        10000.0 ** (-2.0 * jnp.arange(HEAD_DIM // 2).astype(jnp.float32) / HEAD_DIM)
    )
    cosine, sine = jnp.cos(angles)[:, None, :], jnp.sin(angles)[:, None, :]
    local_width = w_qkv.shape[2]
    heads_here = local_width // HEAD_DIM
    out_width = w_out.shape[1]
    hidden_width = w_up.shape[1]
    bits = high_bits()
    across = (((1,), (1,)), ((), ()))

    first_bits, last_bit = bits[:-1], bits[-1]

    def gather_first_z(part):
        for bit in first_bits:
            got = swap(part, bit)
            part = mark(jnp.concatenate(step(part, got), axis=1))
        return part

    def gather_last_z(part, got):
        return mark(jnp.concatenate(step(part, got), axis=1))

    def cut_z(terms):
        cut = terms[0].shape[1] // 2
        away = low(add_low(*[t[:, cut:] for t in terms]))
        return away, [t[:, :cut] for t in terms]

    def add_all_z(away, kept):
        terms = kept + [swap(away, last_bit)]
        for bit in first_bits[::-1]:
            away, kept = cut_z(list(step(*terms)))
            mark(away)
            terms = kept + [swap(away, bit)]
        return terms

    to_rel = relative_map(members, width)

    def relative(values):
        return jnp.dot(values, to_rel, preferred_element_type=jnp.float32)

    def absolute(values, precision=None):
        return lax.dot_general(
            values,
            to_rel.astype(values.dtype),
            (((1,), (1,)), ((), ())),
            precision=precision,
            preferred_element_type=jnp.float32,
        )

    def both(mine, got):
        return jnp.concatenate([mine, got], axis=0)

    def swap_rows(values):
        if groups == 2:
            return values, swap_core(values)
        every = lax.all_gather(values, "tensor", axis=0, tiled=True)
        return every, every[:0]

    one = as_halves(w_qkv.reshape(w_qkv.shape[0], 3 * local_width))
    two = as_halves(jnp.concatenate([w_out, w_up], axis=1))
    three_a, three_b = as_halves(w_down)
    three_got = swap(three_a, 0), swap(three_b, 1)
    one_a, one_b = one[:1], one[1:]
    counted = [jnp.sum(lengths).astype(jnp.float32).reshape(1, 1)]
    to_count = [0, bits[0], 1, *bits[1:]]

    def count_more():
        total = counted[-1]
        if len(counted) > 1:
            total = mark(sum(step(*counted)))
        counted[:] = [total, swap(total, to_count.pop(0))] if to_count else [total]

    count_more()
    got_a, got_b = swap(one_a, first_bits[0]), swap(one_b, first_bits[0])
    one_a = mark(jnp.concatenate(step(one_a, got_a), axis=1))
    for bit in first_bits[1:]:
        one_a = mark(jnp.concatenate(step(one_a, swap(one_a, bit)), axis=1))
    got_a = swap(one_a, last_bit)
    count_more()
    one_b = mark(jnp.concatenate(step(one_b, got_b), axis=1))
    for bit in first_bits[1:]:
        one_b = mark(jnp.concatenate(step(one_b, swap(one_b, bit)), axis=1))
    got_b = swap(one_b, last_bit)
    count_more()
    tokens, teacher, norm_gain, norm_bias = step(tokens, teacher, norm_gain, norm_bias)
    inputs = relative(tokens)
    target = low(relative(teacher))
    affine = jnp.dot(
        jnp.concatenate([norm_gain, norm_bias], axis=0),
        to_rel.astype(jnp.float32),
        precision=lax.Precision.HIGHEST,
        preferred_element_type=jnp.float32,
    )
    gain, bias = affine[:4], affine[4:]
    normal_zero, inv_zero = norm_stats(inputs)
    rows_one, other_one = swap_rows(mark(low(normal_zero * gain[0] + bias[0])))
    one = step(one_a, got_a, one_b, got_b)
    one = mark(jnp.concatenate([as_rows(p) for p in one], axis=0))
    one_x, one_y = swap(one, 0), swap(one, 1)
    count_more()
    two = step(two)
    for bit in first_bits[:1]:
        two_got = swap(two, bit)
    three_a, three_b, three_xa, three_yb = step(three_a, three_b, *three_got)
    three_a, three_b = mark(jnp.stack([three_a, three_xa]), jnp.stack([three_b, three_yb]))
    two = mark(jnp.concatenate(step(two, two_got), axis=1))
    for bit in first_bits[1:]:
        two = mark(jnp.concatenate(step(two, swap(two, bit)), axis=1))
    two_got = swap(two, last_bit)
    three_a = step(three_a)
    three_got_a = swap(three_a, first_bits[0])

    def high_steps(part, got):
        part = mark(jnp.concatenate(step(part, got), axis=1))
        for bit in first_bits[1:]:
            part = mark(jnp.concatenate(step(part, swap(part, bit)), axis=1))
        return part, swap(part, last_bit)

    cut = one.shape[0] // 2
    one_x, one_y = step(one_x, one_y)
    corner_a, corner_b = mark(one_x[:cut], one_y[cut:])
    corner_a, corner_b = swap(corner_a, 1), swap(corner_b, 0)
    two = mark(as_rows(jnp.concatenate(step(two, two_got), axis=1)))
    two_x, two_y = swap(two, 0), swap(two, 1)
    three_b = step(three_b)
    three_got = three_got_a, swap(three_b, first_bits[0])
    one, other_one, corner_a, corner_b = step(one, other_one, corner_a, corner_b)
    weight_qkv = join_rows(one, one_x, one_y, corner_a, corner_b)
    rows_one = both(rows_one, other_one)
    mixed = jnp.dot(rows_one, weight_qkv, preferred_element_type=jnp.float32)
    mixed = mixed.reshape(row_count, slot_count, 3, heads_here, HEAD_DIM)
    queries = low(rotate_pairs(mixed[:, :, 0], cosine, sine))
    key_rows = low(rotate_pairs(mixed[:, :, 1], cosine, sine))
    value_rows = low(mixed[:, :, 2])
    attended, totals = lax.map(
        attend_forward, (queries, key_rows, value_rows, lengths, row_places)
    )
    attended_low = mark(low(attended.reshape(group_tokens, local_width)))
    while len(counted) > 1:
        count_more()
    weight = valid * (all_slots / counted[0])
    three_a, got_a = high_steps(three_a, three_got[0])
    three_b, got_b = high_steps(three_b, three_got[1])
    two_x, two_y = step(two_x, two_y)
    corner_a, corner_b = mark(two_x[:cut], two_y[cut:])
    corner_a, corner_b = swap(corner_a, 1), swap(corner_b, 0)
    three_a, three_b = gather_last_z(three_a, got_a), gather_last_z(three_b, got_b)
    last_a, last_b = swap(three_a, 1), swap(three_b, 0)
    two, corner_a, corner_b = step(two, corner_a, corner_b)
    weight_mid = mark(join_rows(two, two_x, two_y, corner_a, corner_b))
    weight_out, weight_up = weight_mid[:, :out_width], weight_mid[:, out_width:]
    attn_mine, attn_got = product_reduce(attended_low, weight_out, across)
    mark(attn_mine)
    attn_sum = add_low(*step(attn_mine, attn_got))
    normal_one, inv_one = norm_stats(attn_sum)
    middle = inputs + normal_one * gain[1] + bias[1]
    normal_two, inv_two = norm_stats(middle)
    rows_two, other_two = swap_rows(mark(low(normal_two * gain[2] + bias[2])))
    rows_two = both(*step(rows_two, other_two))
    hidden = jnp.dot(rows_two, weight_up, preferred_element_type=jnp.float32)
    half = 0.5 * (1.0 + lax.erf(hidden * (2.0**-0.5)))
    active = low(hidden * half)
    slope = low(half + hidden * jnp.exp(-0.5 * hidden * hidden) * ((2.0 * jnp.pi) ** -0.5))
    active, slope = mark(*lax.optimization_barrier((active, slope)))
    (y_a0, y_a1), (x_b0, x_b1) = step(last_a, last_b)
    weight_down = mark(
        join_rows(three_a[0], three_b[0], three_a[1], x_b0, y_a0, three_b[1], y_a1, x_b1)
    )
    mine, got = product_reduce(active, weight_down, across)
    mark(mine)
    mine, got = step(mine, jnp.broadcast_to(got, mine.shape))
    result, out_grad, mlp_grad, last_sums = last_norm(
        mine, got, middle, target, weight, gain[3:4], bias[3:4]
    )
    mlp_rows, other = swap_rows(mark(mlp_grad))
    mlp_rows = both(*step(mlp_rows, other))

    def down_block(k):
        return mark(product_t(columns(step(mlp_rows), k), active))

    away = down_block(4), down_block(3)
    early = swap(away[0], 1), swap(away[1], 0)
    away = down_block(6), down_block(7)
    late = swap(away[0], 1), swap(away[1], 0)
    active_grad = jnp.dot(step(mlp_rows), weight_down, preferred_element_type=jnp.float32)
    hidden_grad = mark(low(active_grad * slope.astype(jnp.float32)))
    two_mine, two_got = product_reduce(hidden_grad, weight_mid, across, out_width)
    mark(two_mine)
    block = mark(product_t(quarter(step(rows_two), 3), hidden_grad))
    early = step(*early)
    corner_a, corner_b = swap(block[:cut], 1), swap(block[cut:], 0)
    kept = [down_block(k) for k in (0, 2, 1, 5)]
    normed_two_grad = add_low(*step(two_mine, two_got))
    middle_extra, gain_two, bias_two = norm_back(normed_two_grad, normal_two, inv_two, gain[2])
    middle_grad = out_grad + middle_extra
    attn_grad, gain_one, bias_one = norm_back(middle_grad, normal_one, inv_one, gain[1])
    attn_rows, other = swap_rows(mark(low(attn_grad)))
    def up_block(k):
        return mark(product_t(columns(step(rows_two), k), hidden_grad))

    side_b, side_a = up_block(3), up_block(4)
    two_xb, two_ya = swap(side_b, 0), swap(side_a, 1)
    side_a, side_b = up_block(2), up_block(5)
    two_here = mark(product_t(quarter(step(rows_two), 0), hidden_grad))
    late = step(*late)
    down = jnp.stack(
        [low(add_low(k, g)) for k, g in zip(kept, (early[0], late[0], early[1], late[1]))], axis=0
    )
    down_away, down_kept = cut_z([down])
    mark(down_away)
    down_got = swap(down_away, last_bit)
    queries_now, totals_now = step(queries, totals)
    probs_low = [
        attend_probs(
            tuple(v[row] for v in (queries_now, key_rows, totals_now, lengths, row_places))
        )
        for row in range(row_count)
    ]
    mark(*[p for row in probs_low for p in row])
    attn_rows = both(*step(attn_rows, other))
    attended_grad = mark(
        low(jnp.dot(attn_rows, weight_out, preferred_element_type=jnp.float32))
    ).reshape(row_count, slot_count, heads_here, HEAD_DIM)

    side_a = mark(low(add_low(side_a, step(corner_a))))
    side_b = mark(low(add_low(side_b, step(corner_b))))
    two_xa, two_yb = swap(side_a, 0), swap(side_b, 1)
    grads = [
        attend_backward(
            tuple(v[row] for v in (queries, key_rows, value_rows, attended, attended_grad)),
            probs_low[row],
            step,
            mark,
        )
        for row in range(row_count)
    ]
    query_grads, key_grads, value_grads = (jnp.stack(g, axis=0) for g in zip(*grads))
    query_grads, key_grads, value_grads = step(query_grads, key_grads, value_grads)
    mixed_grad = jnp.stack(
        [
            rotate_pairs(query_grads, cosine, -sine),
            rotate_pairs(key_grads, cosine, -sine),
            value_grads,
        ],
        axis=2,
    )
    mixed_grad = mark(low(mixed_grad.reshape(group_tokens, 3 * local_width)))

    def add_corners(over_x, over_y, from_y, from_x):
        over_x = jnp.concatenate([low(add_low(over_x[:cut], from_y)), over_x[cut:]], axis=0)
        over_y = jnp.concatenate([over_y[:cut], low(add_low(over_y[cut:], from_x))], axis=0)
        return mark(over_x, over_y)

    def one_block(k):
        left, right = step(attn_rows, rows_one)
        return mark(
            jnp.concatenate(
                [
                    product_t(quarter(left, k), attended_low),
                    product_t(quarter(right, k), mixed_grad),
                ],
                axis=1,
            )
        )

    block = one_block(3)
    down_got, *down_kept = step(down_got, *down_kept)
    down_away, down_kept = cut_z(down_kept + [down_got])
    mark(down_away)
    for bit in first_bits[:0:-1]:
        down_away, down_kept = cut_z(down_kept + [step(swap(down_away, bit))])
        mark(down_away)
    down_got = swap(down_away, first_bits[0])
    two_xa, two_xb, two_ya, two_yb = step(two_xa, two_xb, two_ya, two_yb)
    corner_a, corner_b = swap(block[:cut], 1), swap(block[cut:], 0)
    two_away, two_kept = cut_z(
        [as_halves(two_here), jnp.stack([two_xa, two_xb]), jnp.stack([two_ya, two_yb])]
    )
    mark(two_away)
    two_got = swap(two_away, last_bit)
    one_mine, one_got = product_reduce(step(mixed_grad), weight_qkv, across)
    mark(one_mine)
    blocks = [one_block(k) for k in (1, 2)]
    over_x, over_y = add_corners(*step(*blocks, corner_a, corner_b))
    one_x, one_y = swap(over_x, 0), swap(over_y, 1)
    one_here = one_block(0)
    normed_one_grad = add_low(*step(one_mine, one_got))
    input_extra, gain_zero, bias_zero = norm_back(normed_one_grad, normal_zero, inv_zero, gain[0])
    inputs_grad = mark(middle_grad + input_extra)
    last_sums = step(last_sums)
    gain_three, bias_three = jnp.sum(last_sums[:8], axis=0), jnp.sum(last_sums[8:16], axis=0)
    squared = jnp.sum(last_sums[16:])
    sums = jnp.stack(
        [
            gain_zero, gain_one, gain_two, gain_three,
            bias_zero, bias_one, bias_two, bias_three,
        ],
        axis=0,
    )
    total = jnp.broadcast_to(squared, (8, 128))
    if groups == 2:
        sums = mark(jnp.concatenate([step(sums), total], axis=1))
        total = swap_core(sums)
    else:
        sums = lax.psum(jnp.concatenate([sums, total], axis=1), "tensor")
        total = jnp.zeros_like(sums)

    def send_sums(sums, total, bit):
        middle_column = sums.shape[1] // 2
        sent = mark(jnp.concatenate([sums[:, middle_column:], total], axis=1))
        return sums[:, :middle_column], total, swap(sent, bit)

    def take_sums(sums, total, got):
        got = step(got)
        return sums + got[:, : sums.shape[1]], total + got[:, sums.shape[1] :]

    two_got, *two_kept = step(two_got, *two_kept)
    two_away, two_kept = cut_z(two_kept + [two_got])
    mark(two_away)
    for bit in first_bits[:0:-1]:
        two_away, two_kept = cut_z(two_kept + [step(swap(two_away, bit))])
        mark(two_away)
    two_got = swap(two_away, first_bits[0])
    down_got, *down_kept = step(down_got, *down_kept)
    down = add_low(*down_kept, down_got)
    down_low = mark(low(down))
    sums, total = step(sums, total)
    sums = sums + total
    pending = send_sums(sums[:, :width], sums[:, width:], 1)
    two_got, *two_kept = step(two_got, *two_kept)
    two = mark(as_rows(add_low(*two_kept, two_got)))
    one_here, one_x, one_y = step(one_here, one_x, one_y)
    sums, total = take_sums(*pending)
    pending = send_sums(sums, total, 0)
    terms = [as_halves(t) for t in step(one_here, one_x, one_y)]
    one_away, one_kept = cut_z(terms)
    mark(one_away)
    sums, total = take_sums(*pending)
    middle_column = sums.shape[1] // 2
    sums = jnp.concatenate([sums[:, :middle_column], sums[:, middle_column:]], axis=0)
    total = jnp.concatenate([total, total], axis=0)

    def with_sums(away):
        sent = jnp.concatenate([sums[:, sums.shape[1] // 2 :], total], axis=1)
        sent = jnp.concatenate([sent[:8], sent[8:]], axis=1)
        high = low(sent)
        sent = jnp.concatenate([high, low(sent - high.astype(jnp.float32))], axis=1)
        columns_there = away.shape[2]
        sent = jnp.pad(sent, ((0, 0), (0, -sent.shape[1] % columns_there)))
        sent = jnp.split(sent, sent.shape[1] // columns_there, axis=1)
        return mark(jnp.concatenate([as_rows(away), *sent], axis=0))

    def take_both(got, rows):
        middle_column = sums.shape[1] // 2
        span = middle_column + total.shape[1]
        extra = got[rows:].astype(jnp.float32)
        extra = jnp.concatenate(jnp.split(extra, extra.shape[0] // 8, axis=0), axis=1)
        extra = extra[:, : 2 * span] + extra[:, 2 * span : 4 * span]
        extra = jnp.concatenate([extra[:, :span], extra[:, span:]], axis=0)
        return (
            got[:rows][None],
            sums[:, :middle_column] + extra[:, :middle_column],
            total + extra[:, middle_column:],
        )

    away_a, away_b = one_away[:1], one_away[1:]
    one_kept = mark(low(add_low(*one_kept)))
    kept_a, kept_b = [one_kept[:1]], [one_kept[1:]]
    got_a = swap(with_sums(away_a), last_bit)
    got_b = swap(mark(step(away_b)), last_bit)
    down_low = step(down_low)
    down_got = swap(down_low[1], 0), swap(down_low[3], 1)
    inputs_grad = step(inputs_grad)
    tokens_grad = mark(absolute(inputs_grad, lax.Precision.HIGHEST))
    for bit in first_bits[::-1]:
        got_a, *kept_a = step(got_a, *kept_a)
        got_a, sums, total = take_both(got_a, away_a.shape[1])
        away_a, kept_a = cut_z(kept_a + [got_a])
        got_a = swap(with_sums(away_a), bit)
        got_b, *kept_b = step(got_b, *kept_b)
        away_b, kept_b = cut_z(kept_b + [got_b])
        got_b = swap(mark(away_b), bit)
    layer_output = mark(low(absolute(step(result))))
    down_a, down_b = step(*down_got)
    down_part = mark(jnp.concatenate([add_low(down[0], down_a), add_low(down[2], down_b)], axis=0))
    got_a, *kept_a = step(got_a, *kept_a)
    got_a, sums, total = take_both(got_a, away_a.shape[1])
    got_b, *kept_b = step(got_b, *kept_b)
    small = lax.optimization_barrier(jnp.concatenate([sums[:8], sums[8:], total[:8]], axis=1))
    loss = small[0, small.shape[1] - 1] / (all_slots * width)
    own = width // (members * groups)
    sums = lax.dynamic_slice_in_dim(small, me * own, own, 1)

    def one_part(first):
        lanes = slice(first, first + local_width)
        return as_rows(
            jnp.concatenate(
                [
                    add_low(*[t[..., lanes] for t in kept_a], got_a[..., lanes]),
                    add_low(*[t[..., lanes] for t in kept_b], got_b[..., lanes]),
                ],
                axis=0,
            )
        )

    qkv_part = jnp.stack([one_part(out_width + k * local_width) for k in range(3)], axis=1)
    return (
        loss,
        layer_output,
        tokens_grad,
        qkv_part,
        one_part(0),
        two,
        down_part,
        sums[:4],
        sums[4:],
    )


def solution(mesh):
    return jax.shard_map(
        on_device,
        mesh=mesh,
        in_specs=(
            P(("dp", "tensor"), None),
            P(("dp", "tensor"), None),
            P("dp"),
            P("dp", None, "tensor"),
            P("dp", "tensor"),
            P("dp", "tensor"),
            P("dp", "tensor"),
            P(),
            P(),
        ),
        out_specs=(
            P(),
            P(("dp", "tensor"), None),
            P(("dp", "tensor"), None),
            P("dp", None, "tensor"),
            P("dp", "tensor"),
            P("dp", "tensor"),
            P("dp", "tensor"),
            P(None, ("dp", "tensor")),
            P(None, ("dp", "tensor")),
        ),
        check_vma=False,
    )
```
